32 devices in a mesh: groups: 2 (over x), ctx: 16 (over z, y, core).
Axes of the slice: x: 2, y: 2, z: 4, core: 2. Of those that a mesh axis runs over, the one named last changes fastest.
Arguments:
- features: bfloat16 [8192, 3, 4096], P(('groups', 'ctx')), parts along dimension 0, may hold values from -6 to 6
- short_weight: float32 [3, 3, 4096], replicated, may hold values from -3 to 3
- residues: float32 [256, 16], replicated, may hold values from -4 to 4
- rates: float32 [256, 16], replicated, may hold values from 0 to 1, as said below
- skip: float32 [4096], replicated, may hold values from -4 to 4
- carry_state: float32 [32, 4096], P('groups'), parts along dimension 0, may hold values from -120 to 120
- earlier_rows: bfloat16 [4, 3, 4096], P('groups'), parts along dimension 0, may hold values from -6 to 6
- segment_ids: int32 [8192], P('groups'), parts along dimension 0, may hold values from 0 to 7, never falling along the last dimension, each value on 1 to 3072 neighbouring positions
Outputs:
- mixed: bfloat16 [8192, 4096], P(('groups', 'ctx')), parts along dimension 0
The draws below stay inside these ranges and needn't reach their ends.
There are 2 independent parts, one for each index of `groups`. The reference program is written for one: setup_inputs(seed, part) draws one part's arguments, and reference() takes and returns one part's arrays. A program takes and returns all parts, laid end to end along the dimension named above; an argument that names none is the same for every part. Nothing has to cross between parts.
Inputs may be any that keep to these rules, and one draw needn't show every extreme that they name: Positive decay rates, at most 1 / 30. `segment_ids`: never falling, starting at record 0, which continues the record that closes the earlier span; each record holds at most 3072 tokens, one exactly that many.
All inputs are finite; a program needn't handle non-finite values.
Results may differ from the reference program's by a relative error of at most 0.0065.
Values may be sent and summed in bfloat16 or wider, within the bound.
No kernel may reach another device: no remote copies, remote signals or barrier semaphores. Data moves between devices by JAX's collectives and lax.ppermute only.
A program may use at most 128 MiB of HBM per device.

```python
import math
import jax
import jax.numpy as jnp
import numpy as np
from jax import lax

CH = 4096
FG = 16
MODES = 16
TAPS = 3
SEGS = 8
TOK_DEV = 256
GRP = 256
SEQ = 4096
N_CTX = 16


def draw_rates(key, part):
    key_slow, key_fast, key_pick = jax.random.split(jax.random.fold_in(key, 17), 3)
    shape = (CH // FG, MODES)
    slow = jnp.exp(jax.random.uniform(key_slow, shape, jnp.float32, jnp.log(0.2 / SEQ), jnp.log(2.0 / SEQ)))
    fast = jnp.exp(jax.random.uniform(key_fast, shape, jnp.float32, jnp.log(1.0 / 50.0), jnp.log(1.0 / 30.0)))
    share = 0.5
    pick = jax.random.uniform(key_pick, shape, jnp.float32) < share
    return jnp.where(pick, slow, fast).astype(jnp.float32)


def block_levels(rng, shape, cuts, low, top_value):
    loudness, own = 1.0, jax.random.fold_in(rng, 6)
    for axis_at, parts in cuts:
        draws = jnp.exp(jax.random.uniform(jax.random.fold_in(own, axis_at), (parts,), jnp.float32, low / len(cuts), top_value / len(cuts)))
        loudness = loudness * jnp.repeat(draws, shape[axis_at] // parts).reshape([-1 if axis == axis_at else 1 for axis in range(len(shape))])
    return loudness


def split_up(count, total, bound, slope):
    portions = [(1 << 20) // math.isqrt(grade ** slope) + 1 for grade in range(2, count + 1)]
    surplus, holding = total - bound - (count - 1), [1] * (count - 1)
    while surplus > 0:
        candidates = [i for i in range(count - 1) if holding[i] < bound]
        whole, budget = sum([portions[i] for i in candidates]), surplus
        for i in candidates:
            more = min(bound - holding[i], max(1, budget * portions[i] // whole), surplus)
            holding[i] = holding[i] + more
            surplus = surplus - more
    return np.array([bound] + holding)


def ragged(rng, count, total, bound, skew):
    if count == 2:
        one = jax.random.randint(rng, (), max(1, total - bound), min(bound, total - 1) + 1)
        return jnp.stack([one, total - one])
    lengths = jnp.asarray(split_up(count, total, bound, skew), jnp.int32)
    twos = (count - 1) // 2
    source_of, sink = lengths[1:1 + 2 * twos:2], lengths[2:2 + 2 * twos:2]
    margin = jnp.minimum(source_of - 1, bound - sink)
    shifted = jax.random.randint(jax.random.fold_in(rng, 1), (twos,), 0, 1 << 20) % (margin + 1)
    lengths = lengths.at[1:1 + 2 * twos:2].set(source_of - shifted).at[2:2 + 2 * twos:2].set(sink + shifted)
    return lengths[jax.random.permutation(jax.random.fold_in(rng, 2), count)]


def gaussian(key, extent, scale, bound, pieces=(), dtype=jnp.bfloat16):
    entries = scale * jax.random.normal(key, extent, jnp.float32)
    if pieces:
        entries = entries * block_levels(key, extent, pieces, -0.22, 0.18)
    return jnp.clip(entries, -bound, bound).astype(dtype)


def setup_inputs(seed: int = 0, part: int = 0) -> dict:
    streams_of = jax.random.split(jax.random.key(seed), 9)
    part_splits = jax.random.split(jax.random.fold_in(streams_of[8], part), 9)
    features = gaussian(part_splits[0], (SEQ, 3, CH), 1.0, 6.0, ((0, 16),))
    short_weight = gaussian(streams_of[1], (TAPS, 3, CH), 0.6, 3.0, (), jnp.float32)
    residues = gaussian(streams_of[2], (GRP, MODES), 1.0, 4.0, (), jnp.float32)
    rates = draw_rates(jax.random.fold_in(streams_of[8], 71), part)
    skip = gaussian(streams_of[4], (CH,), 1.0, 4.0, (), jnp.float32)
    carry_state = gaussian(part_splits[5], (MODES, CH), 20.0, 120.0, (), jnp.float32)
    earlier_rows = gaussian(part_splits[6], (2, 3, CH), 1.0, 6.0)
    segment_ids = jnp.searchsorted(jnp.cumsum(ragged(part_splits[7], SEGS, SEQ, SEQ - SEQ // 4, 2)), jnp.arange(SEQ), side="right").astype(jnp.int32)
    return {"features": features, "short_weight": short_weight, "residues": residues, "rates": rates, "skip": skip, "carry_state": carry_state, "earlier_rows": earlier_rows, "segment_ids": segment_ids}


def short_filter(rows_ext, short_weight, seg_ext):
    count = rows_ext.shape[0] - 2
    total = jnp.zeros((count,) + rows_ext.shape[1:], jnp.float32)
    for offset in range(short_weight.shape[0]):
        begin = 2 - offset
        piece = rows_ext[begin:begin + count].astype(jnp.float32)
        keep = seg_ext[begin:begin + count] == seg_ext[2:]
        total = total + short_weight[offset][None] * jnp.where(keep[:, None, None], piece, jnp.float32(0.0))
    return total

def lag_table(residues, rates, count):
    lags = jnp.arange(count).astype(jnp.float32)
    weight_mode = residues * jnp.sqrt(rates)
    return lax.optimization_barrier(jnp.sum(weight_mode[:, :, None] * jnp.exp(-rates[:, :, None] * lags[None, None, :]), axis=1))

def toeplitz(table):
    count = table.shape[1]
    flipped = jnp.concatenate([table[:, ::-1], jnp.zeros_like(table)], axis=1)
    tiled = jnp.tile(flipped, (1, count + 1))
    window = tiled[:, count - 1:count - 1 + count * (2 * count - 1)]
    return window.reshape(table.shape[0], count, 2 * count - 1)[:, :, :count]

def local_conv(u_block, seg_blk, table):
    count, width = u_block.shape
    groups = table.shape[0]
    members = width // groups
    step_groups = min(groups, 16)
    rounds = groups // step_groups
    same = seg_blk[:, None] == seg_blk[None, :]
    grouped = u_block.reshape(count, rounds, step_groups, members).transpose(1, 0, 2, 3)
    tables = table.reshape(rounds, step_groups, count)

    def one_step(pair):
        tab, values = pair
        matrix = jnp.where(same[None], toeplitz(tab), jnp.float32(0.0))
        matrix = lax.optimization_barrier(matrix.astype(jnp.bfloat16)).astype(jnp.float32)
        return jnp.einsum('gts,sgf->tgf', matrix, values.astype(jnp.float32), precision=lax.Precision.HIGHEST)
    result = lax.map(one_step, (tables, grouped))
    return result.transpose(1, 0, 2, 3).reshape(count, width)

def block_state(u_block, seg_blk, seg_prev, rates):
    count, width = u_block.shape
    groups = rates.shape[0]
    members = width // groups
    lags_end = (count - 1 - jnp.arange(count)).astype(jnp.float32)
    keep_end = seg_blk == seg_blk[count - 1]
    decay = jnp.where(keep_end[None, None, :], jnp.exp(-rates[:, :, None] * lags_end[None, None, :]), jnp.float32(0.0))
    decay = lax.optimization_barrier(decay.astype(jnp.bfloat16)).astype(jnp.float32)
    grouped = u_block.reshape(count, groups, members).astype(jnp.float32)
    block_sum = jnp.einsum('gms,sgf->mgf', decay, grouped, precision=lax.Precision.HIGHEST)
    factor = jnp.where(seg_prev == seg_blk[count - 1], jnp.exp(-rates * count), jnp.float32(0.0))
    return (factor.T[:, :, None], block_sum)

def cross_term(state_in, seg_blk, seg_prev, residues, rates):
    count = seg_blk.shape[0]
    offsets = jnp.arange(1, count + 1).astype(jnp.float32)
    weights = (residues * jnp.sqrt(rates))[None] * jnp.exp(-rates[None] * offsets[:, None, None])
    weights = jnp.where((seg_blk == seg_prev)[:, None, None], weights, jnp.float32(0.0))
    result = jnp.einsum('tgm,mgf->tgf', weights, state_in, precision=lax.Precision.HIGHEST)
    return result.reshape(count, -1)

def reference(features, short_weight, residues, rates, skip, carry_state, earlier_rows, segment_ids):
    count = TOK_DEV
    groups, modes = rates.shape
    width = features.shape[2]
    members = width // groups
    table = lag_table(residues, rates, count)
    seg_pad = jnp.concatenate([jnp.zeros((2,), jnp.int32), segment_ids.astype(jnp.int32)])
    blocks = features.reshape(N_CTX, count, 3, width)

    def advance(carry, inputs):
        state, previous = carry
        rows, number = inputs
        seg_ext = lax.dynamic_slice(seg_pad, (number * count,), (count + 2,))
        seg_blk = seg_ext[2:]
        seg_prev = seg_ext[1]
        extended = jnp.concatenate([previous, rows], axis=0)
        filtered = short_filter(extended, short_weight, seg_ext)
        u_block = lax.optimization_barrier((filtered[:, 1] * filtered[:, 2]).astype(jnp.bfloat16))
        local = local_conv(u_block, seg_blk, table)
        factor, block_sum = block_state(u_block, seg_blk, seg_prev, rates)
        cross = cross_term(state, seg_blk, seg_prev, residues, rates)
        mixed = (filtered[:, 0] * (local + cross + skip[None] * u_block.astype(jnp.float32))).astype(jnp.bfloat16)
        return ((factor * state + block_sum, rows[count - 2:]), mixed)
    numbers = jnp.arange(N_CTX).astype(jnp.int32)
    start_state = (carry_state.reshape(modes, groups, members), earlier_rows)
    final, outputs = lax.scan(advance, start_state, (blocks, numbers))
    return outputs.reshape(N_CTX * count, width)
```

```python
import functools

import jax
import jax.numpy as jnp
from jax import lax
from jax.experimental import pallas as pl
from jax.experimental.pallas import tpu as pltpu
from jax.sharding import PartitionSpec as P

BF = jnp.bfloat16
F32 = jnp.float32
LANES = 128
SET = 256
HALF = 128


def iota(shape, dim):
    return lax.broadcasted_iota(jnp.int32, shape, dim)


def split3(x):
    hi = x.astype(BF)
    rest = x - hi.astype(F32)
    mid = rest.astype(BF)
    low = (rest - mid.astype(F32)).astype(BF)
    return [hi, mid, low]


def segment_columns(pos, seg_ref):
    halves, rows = [], []
    for part in range(2):
        row = seg_ref[pl.ds(2 * pos + part, 1), :].astype(F32)
        rows.append(row)
        halves.append(jnp.transpose(jnp.broadcast_to(row, (HALF, LANES))))
    before = seg_ref[pl.ds(jnp.maximum(2 * pos - 1, 0), 1), :].astype(F32)
    before = jnp.where(pos == 0, jnp.zeros_like(before), before)
    last = jnp.broadcast_to(before[:, LANES - 1 :], (1, LANES))
    second = jnp.broadcast_to(before[:, LANES - 2 : LANES - 1], (1, LANES))
    return jnp.concatenate(halves, axis=0), rows, last, second


def first_kernel(pos_ref, seg_ref, rates_ref, res_ref, k_ref, v_ref, sw_ref,
                 u_ref, sum_ref, rate_ref, rflat_ref, wflat_ref, col_ref, tri_ref, keep_ref):
    step = pl.program_id(0)
    pos = pos_ref[0]
    count = k_ref.shape[0]
    modes = rates_ref.shape[0]
    members = SET // modes

    @pl.when(step == 0)
    def _():
        col, rows, last, second = segment_columns(pos, seg_ref)
        token = iota((count, LANES), 0)
        one = jnp.where(token == 0, last, pltpu.roll(col, 1, 0))
        two = jnp.where(token == 0, second, jnp.where(token == 1, last, pltpu.roll(col, 2, 0)))
        col_ref[0] = (col == one).astype(F32)
        col_ref[1] = (col == two).astype(F32)
        col_ref[2] = (col == last).astype(F32)
        end = jnp.broadcast_to(rows[1][:, LANES - 1 :], (1, LANES))
        keep_ref[...] = (col == end).astype(F32)
        t = iota((HALF, HALF), 0)
        s = iota((HALF, HALF), 1)
        same = [[col[a * HALF : (a + 1) * HALF] == rows[b] for b in range(2)] for a in range(2)]
        tri_ref[0] = ((t >= s) & same[0][0]).astype(F32).astype(BF)
        tri_ref[1] = ((t >= s) & same[1][0]).astype(F32).astype(BF)
        tri_ref[2] = ((t < s) & same[1][0]).astype(F32).astype(BF)
        tri_ref[3] = ((t >= s) & same[1][1]).astype(F32).astype(BF)

    spot = iota((LANES, SET), 0)
    lane = iota((LANES, SET), 1)
    onehot = (spot == lane // members + members * lax.rem(step, LANES // members)).astype(F32).astype(BF)
    rates = rates_ref[...]
    weight = res_ref[...] * jnp.sqrt(rates)
    spread = jnp.dot(jnp.concatenate(split3(rates) + split3(weight), axis=0), onehot, preferred_element_type=F32)
    rate = (spread[:modes] + spread[modes : 2 * modes]) + spread[2 * modes : 3 * modes]
    wide = (spread[3 * modes : 4 * modes] + spread[4 * modes : 5 * modes]) + spread[5 * modes :]
    rate_ref[...] = rate
    pick = iota((modes, SET), 0) == lax.rem(iota((modes, SET), 1), modes)
    rflat = jnp.sum(jnp.where(pick, rate, 0.0), axis=0, keepdims=True)
    wflat = jnp.sum(jnp.where(pick, wide, 0.0), axis=0, keepdims=True)
    rflat_ref[...] = rflat
    wflat_ref[...] = wflat

    token = iota((count, LANES), 0)
    one = col_ref[0]
    two = col_ref[1]
    pieces = []
    for half in range(SET // LANES):
        at = slice(half * LANES, (half + 1) * LANES)
        made = []
        for index, ref in ((1, k_ref), (2, v_ref)):
            x = ref[:, at].astype(F32)
            made.append(
                sw_ref[index, 0:1, at] * x
                + sw_ref[index, 1:2, at] * (one * pltpu.roll(x, 1, 0))
                + sw_ref[index, 2:3, at] * (two * pltpu.roll(x, 2, 0))
            )
        pieces.append(jnp.where(token < 2, 0.0, made[0] * made[1]).astype(BF))
    u = jnp.concatenate(pieces, axis=1)
    u_ref[...] = u

    fine = iota((16, SET), 0).astype(F32)
    coarse = jnp.exp(-rflat * (count - 16.0 - 16.0 * fine))
    fine = jnp.exp(-rflat * (15.0 - fine))
    keep = keep_ref[...]
    keep = jnp.concatenate([keep] * (SET // LANES), axis=1)
    decay = jnp.concatenate([coarse[a : a + 1] * fine for a in range(count // 16)], axis=0)
    decay = (decay * keep).astype(BF)
    sums = lax.dot_general(decay, u, (((0,), (0,)), ((), ())), preferred_element_type=F32)
    owner = iota((modes, SET), 1) // members
    total = jnp.zeros((modes, SET), F32)
    for g in range(SET // members):
        total = jnp.where(owner == g, sums[g * modes : (g + 1) * modes], total)
    sum_ref[...] = total


def head_kernel(pos_ref, seg_ref, feat_ref, halo_ref, sw_ref, rate_ref, sum_ref, total_ref, head_ref):
    pos = pos_ref[0]
    width = rate_ref.shape[1]
    count = 2 * LANES
    row = seg_ref[pl.ds(2 * pos, 1), :].astype(F32)
    tail = seg_ref[pl.ds(2 * pos + 1, 1), :].astype(F32)
    before = seg_ref[pl.ds(jnp.maximum(2 * pos - 1, 0), 1), :].astype(F32)
    before = jnp.where(pos == 0, jnp.zeros_like(before), before)
    s0, s1 = row[:, 0:1], row[:, 1:2]
    end = tail[:, LANES - 1 :]
    p1, p2 = before[:, LANES - 1 :], before[:, LANES - 2 : LANES - 1]

    def same(a, b):
        return jnp.broadcast_to((a == b).astype(F32), (1, width))

    made = []
    for index in (1, 2):
        x = feat_ref[index].astype(F32)
        h = halo_ref[index].astype(F32)
        x0, x1 = x[0:1], x[1:2]
        h2, h1 = h[0:1], h[1:2]
        w = [sw_ref[index, j : j + 1, :] for j in range(3)]
        f0 = w[0] * x0 + w[1] * (same(p1, s0) * h1) + w[2] * (same(p2, s0) * h2)
        f1 = w[0] * x1 + w[1] * (same(s0, s1) * x0) + w[2] * (same(p1, s1) * h1)
        made.append((f0, f1))
    u0 = (made[0][0] * made[1][0]).astype(BF).astype(F32)
    u1 = (made[0][1] * made[1][1]).astype(BF).astype(F32)
    head_ref[0:1, :] = u0
    head_ref[1:2, :] = u1
    rate = rate_ref[...]
    total = sum_ref[...]
    total = total + jnp.exp(-rate * (count - 1.0)) * (same(s0, end) * u0)
    total = total + jnp.exp(-rate * (count - 2.0)) * (same(s1, end) * u1)
    half = width // 2
    total_ref[0] = total[:, :half].astype(BF)
    total_ref[1] = total[:, half:].astype(BF)


def local_kernel(u_ref, head_ref, q_ref, halo_ref, sw_ref, skip_ref, rates_ref, res_ref, rflat_ref, wflat_ref,
                 col_ref, tri_ref, out_ref, gate_ref, cross_ref, top_ref, low_ref, rhs_ref):
    count = u_ref.shape[0]
    modes = rates_ref.shape[1]
    members = LANES // rates_ref.shape[0]
    groups = rates_ref.shape[0]
    rates = rates_ref[...]
    weight = res_ref[...] * jnp.sqrt(rates)
    lane = iota((groups, LANES), 1)
    lag = jnp.where(lane == 0, 0, LANES - lane).astype(F32)
    near = jnp.zeros((groups, LANES), F32)
    far = jnp.zeros((groups, LANES), F32)
    for m in range(modes):
        r = rates[:, m : m + 1]
        table = weight[:, m : m + 1] * jnp.exp(-r * lag)
        near = near + table
        far = far + weight[:, m : m + 1] * jnp.exp(-r * (lag + LANES))
    token = iota((count, LANES), 0)
    u = u_ref[...].astype(F32)
    u = jnp.where(token == 0, head_ref[0:1, :], jnp.where(token == 1, head_ref[1:2, :], u))
    ub = u.astype(BF)
    owner = iota((1, LANES), 1) // members
    for g in range(groups):
        first = pltpu.roll(jnp.broadcast_to(near[g : g + 1], (HALF, LANES)), 0, 1, stride=1, stride_axis=0).astype(BF)
        second = pltpu.roll(jnp.broadcast_to(far[g : g + 1], (HALF, LANES)), 0, 1, stride=1, stride_axis=0).astype(BF)
        at = slice(g * HALF, (g + 1) * HALF)
        top_ref[0:HALF, at] = first * tri_ref[0]
        top_ref[HALF:, at] = second * tri_ref[1] + first * tri_ref[2]
        low_ref[:, at] = first * tri_ref[3]
        mine = jnp.broadcast_to((owner == g).astype(F32), (HALF, LANES)).astype(BF)
        rhs_ref[g * HALF : (g + 1) * HALF, :] = ub[:HALF] * mine
        rhs_ref[(groups + g) * HALF : (groups + g + 1) * HALF, :] = ub[HALF:] * mine
    depth = groups * HALF
    upper = jnp.dot(top_ref[...], rhs_ref[:depth, :], preferred_element_type=F32)
    lower = jnp.dot(low_ref[...], rhs_ref[depth:, :], preferred_element_type=F32)
    x = q_ref[...].astype(F32)
    h = halo_ref[...].astype(F32)
    one = jnp.where(token == 0, h[1:2], pltpu.roll(x, 1, 0))
    two = jnp.where(token == 0, h[0:1], jnp.where(token == 1, h[1:2], pltpu.roll(x, 2, 0)))
    q = sw_ref[0, 0:1] * x + sw_ref[0, 1:2] * (col_ref[0] * one) + sw_ref[0, 2:3] * (col_ref[1] * two)
    gate_ref[...] = q
    base = skip_ref[...] * u
    out_ref[:HALF] = q[:HALF] * (upper[:HALF] + base[:HALF])
    out_ref[HALF:] = q[HALF:] * (upper[HALF:] + lower + base[HALF:])
    rflat = rflat_ref[...]
    fine = iota((16, LANES), 0).astype(F32)
    coarse = wflat_ref[...] * jnp.exp(-rflat * (16.0 * fine))
    fine = jnp.exp(-rflat * (fine + 1.0))
    table = jnp.concatenate([coarse[a : a + 1] * fine for a in range(count // 16)], axis=0)
    cross_ref[...] = (table * col_ref[2]).astype(BF)


def last_kernel(state_ref, table_ref, gate_ref, part_ref, out_ref):
    modes = state_ref.shape[0]
    groups = SET // modes
    state = state_ref[...]
    owner = iota((modes, SET), 1) // (SET // groups)
    spread = jnp.concatenate([jnp.where(owner == g, state, 0.0).astype(BF) for g in range(groups)], axis=0)
    cross = jnp.dot(table_ref[...], spread, preferred_element_type=F32)
    out_ref[...] = (part_ref[...] + gate_ref[...] * cross).astype(BF)


def params(limit=None):
    return pltpu.CompilerParams(vmem_limit_bytes=limit or (16 << 20))


def fixed(shape):
    return pl.BlockSpec(shape, lambda i, *_: (0,) * len(shape))


def body(features, short_weight, residues, rates, skip, carry_state, earlier_rows, segment_ids):
    count, _, width = features.shape
    groups, modes = rates.shape
    blocks = lax.axis_size("ctx")
    pos = lax.axis_index("ctx")
    pos1 = pos.reshape(1)
    feat = jnp.transpose(features, (1, 0, 2))
    taps = jnp.transpose(short_weight, (1, 0, 2))
    segs = segment_ids.reshape(-1, LANES)
    rates_t = rates.T
    res_t = residues.T
    skip = skip.reshape(1, width)

    halo = lax.ppermute(feat[:, count - 2 :], "ctx", [(i, i + 1) for i in range(blocks - 1)])
    halo = jnp.where(pos == 0, jnp.transpose(earlier_rows, (1, 0, 2)), halo)

    sets = width // SET
    per = LANES // (groups // sets)
    lane_out = lambda rows, dt: jax.ShapeDtypeStruct((rows, width), dt)
    lane_spec = lambda rows, size: pl.BlockSpec((rows, size), lambda i, *_: (0, i))
    u, sums, rate, rflat, wflat, cols, tris = pl.pallas_call(
        first_kernel,
        grid_spec=pltpu.PrefetchScalarGridSpec(
            num_scalar_prefetch=1,
            grid=(sets,),
            in_specs=[
                fixed(segs.shape),
                pl.BlockSpec((modes, LANES), lambda i, *_: (0, i // per)),
                pl.BlockSpec((modes, LANES), lambda i, *_: (0, i // per)),
                pl.BlockSpec((None, count, SET), lambda i, *_: (1, 0, i)),
                pl.BlockSpec((None, count, SET), lambda i, *_: (2, 0, i)),
                pl.BlockSpec((3, 3, SET), lambda i, *_: (0, 0, i)),
            ],
            out_specs=[
                lane_spec(count, SET),
                lane_spec(modes, SET),
                lane_spec(modes, SET),
                lane_spec(1, SET),
                lane_spec(1, SET),
                fixed((3, count, LANES)),
                fixed((4, HALF, HALF)),
            ],
            scratch_shapes=[pltpu.VMEM((count, LANES), F32)],
        ),
        out_shape=[
            lane_out(count, BF),
            lane_out(modes, F32),
            lane_out(modes, F32),
            lane_out(1, F32),
            lane_out(1, F32),
            jax.ShapeDtypeStruct((3, count, LANES), F32),
            jax.ShapeDtypeStruct((4, HALF, HALF), BF),
        ],
        compiler_params=params(),
        name="first",
    )(pos1, segs, rates_t, res_t, feat, feat, taps)

    vm = pl.BlockSpec(memory_space=pltpu.VMEM)
    total, head = pl.pallas_call(
        head_kernel,
        in_specs=[pl.BlockSpec(memory_space=pltpu.SMEM)] + [vm] * 6,
        out_specs=[vm, vm],
        out_shape=[jax.ShapeDtypeStruct((2, modes, width // 2), BF), lane_out(2, F32)],
        compiler_params=params(),
        name="head",
    )(pos1, segs, feat[:, :2], halo, taps, rate, sums)

    def local(piece, pieces, u):
        tiles = width // LANES // pieces
        first = piece * tiles
        size = tiles * LANES
        per_tile = groups // (width // LANES)
        spec = lambda rows: pl.BlockSpec((rows, LANES), lambda i: (0, first + i))
        mine = lambda rows: pl.BlockSpec((rows, LANES), lambda i: (0, i))
        return pl.pallas_call(
            local_kernel,
            grid=(tiles,),
            in_specs=[
                spec(count),
                spec(2),
                pl.BlockSpec((None, count, LANES), lambda i: (0, 0, first + i)),
                pl.BlockSpec((None, 2, LANES), lambda i: (0, 0, first + i)),
                pl.BlockSpec((3, 3, LANES), lambda i: (0, 0, first + i)),
                spec(1),
                pl.BlockSpec((per_tile, modes), lambda i: (first + i, 0)),
                pl.BlockSpec((per_tile, modes), lambda i: (first + i, 0)),
                spec(1),
                spec(1),
                fixed((3, count, LANES)),
                fixed((4, HALF, HALF)),
            ],
            out_specs=[mine(count), mine(count), mine(count)],
            out_shape=[
                jax.ShapeDtypeStruct((count, size), F32),
                jax.ShapeDtypeStruct((count, size), F32),
                jax.ShapeDtypeStruct((count, size), BF),
            ],
            scratch_shapes=[
                pltpu.VMEM((count, per_tile * HALF), BF),
                pltpu.VMEM((HALF, per_tile * HALF), BF),
                pltpu.VMEM((2 * per_tile * HALF, LANES), BF),
            ],
            compiler_params=params(),
            cost_estimate=pl.CostEstimate(flops=tiles * 2 * 400 * 1024 * 256, bytes_accessed=tiles * 600000, transcendentals=0),
            name="local",
        )(u, head, feat, halo, taps, skip, rates, residues, rflat, wflat, cols, tris)

    ends = segment_ids.reshape(blocks, count)[:, count - 1]
    at_end = lambda b: jnp.where(b < 0, 0, lax.dynamic_index_in_dim(ends, jnp.maximum(b, 0), 0, keepdims=False))
    def decay(rate, low, high):
        alive = at_end(low - 1) == at_end(high - 1)
        return jnp.where(alive, jnp.exp(-rate * (count * (high - low)).astype(F32)), 0.0)

    core = pos % 2
    chip = pos // 2
    chips = blocks // 2
    rate2 = rate.reshape(modes, 2, width // 2)
    rate_half = jnp.where(core == 0, rate2[:, 0], rate2[:, 1])
    swap = lambda value: lax.ppermute(value, "ctx", [(i, i ^ 1) for i in range(blocks)])
    pieces = 4
    parts = []
    other = swap(total)
    low_total = jnp.where(core == 0, total, other)
    own_half = lambda value: jnp.where(core == 0, value[0], value[1]).astype(F32)
    t_low = own_half(low_total)
    t_high = own_half(jnp.where(core == 0, other, total))
    chip_total = decay(rate_half, 2 * chip + 1, 2 * chip + 2) * t_low + t_high
    before = jnp.zeros_like(chip_total)
    reach = 1
    while reach < chips:
        sent = chip_total.astype(BF)
        got = lax.ppermute(sent, "ctx", [(i, i ^ (2 * reach)) for i in range(blocks)]).astype(F32)
        base = (chip // reach) * reach
        upper = (chip // reach) % 2 == 1
        mate = jnp.where(upper, base - reach, base + reach)
        before = before + jnp.where(upper, decay(rate_half, 2 * base, 2 * chip), 0.0) * got
        own = jnp.where(upper, 1.0, decay(rate_half, 2 * mate, 2 * mate + 2 * reach))
        theirs = jnp.where(upper, decay(rate_half, 2 * base, 2 * base + 2 * reach), 1.0)
        chip_total = own * chip_total + theirs * got
        reach *= 2
    mine = before.astype(BF)
    yours = swap(mine)
    full = jnp.concatenate([jnp.where(core == 0, mine, yours), jnp.where(core == 0, yours, mine)], axis=1).astype(F32)
    low_full = jnp.concatenate([low_total[0], low_total[1]], axis=1).astype(F32)
    state = jnp.where(core == 0, full, decay(rate, 2 * chip, 2 * chip + 1) * full + low_full)
    state = state + decay(rate, 0, pos) * carry_state
    for piece in range(pieces):
        parts.append(local(piece, pieces, u))

    outs = []
    size = width // pieces
    done = []
    for piece in range(pieces):
        part, gate, table = parts[piece]
        n = size // SET
        spec = lambda rows: pl.BlockSpec((rows, SET), lambda i: (0, i))
        done.append(pl.pallas_call(
            last_kernel,
            grid=(n,),
            in_specs=[pl.BlockSpec((modes, SET), lambda i, piece=piece: (0, piece * n + i)), spec(count), spec(count), spec(count)],
            out_specs=spec(count),
            out_shape=jax.ShapeDtypeStruct((count, size), BF),
            compiler_params=params(),
            name="last",
        )(state, table, gate, part))
    return jnp.concatenate(done, axis=1)


def solution(mesh):
    placed = (
        P(("groups", "ctx"), None, None),
        P(),
        P(),
        P(),
        P(),
        P("groups", None),
        P("groups", None, None),
        P("groups"),
    )
    return jax.shard_map(
        body, mesh=mesh, in_specs=placed, out_specs=P(("groups", "ctx"), None), check_vma=False
    )
```

```python
import jax
import jax.numpy as jnp
from jax import lax
from jax.experimental import pallas as pl
from jax.experimental.pallas import tpu as pltpu
from jax.sharding import PartitionSpec as P

BF = jnp.bfloat16
F32 = jnp.float32
LANES = 128
SET = 256
WIDE = 1024
SUB = 32


def iota(shape, dim):
    return lax.broadcasted_iota(jnp.int32, shape, dim)


def flag(x):
    return x.astype(F32)


def split3(x):
    hi = x.astype(BF)
    rest = x - hi.astype(F32)
    mid = rest.astype(BF)
    low = (rest - mid.astype(F32)).astype(BF)
    return [hi, mid, low]


def spread_out(values, onehot):
    rows = values[0].shape[0]
    pieces = sum([split3(value) for value in values], [])
    got = jnp.dot(jnp.concatenate(pieces, axis=0), onehot, preferred_element_type=F32)
    part = lambda i: got[i * rows : (i + 1) * rows]
    return [(part(3 * i) + part(3 * i + 1)) + part(3 * i + 2) for i in range(len(values))]


def plan_kernel(count, rounds, pos_ref, seg_ref, ids_ref, rates_ref, res_ref,
                rate_ref, flat_ref, col_ref, tri_ref, keep_ref, half_ref, full_ref):
    pos = pos_ref[0]
    modes = rates_ref.shape[0]
    width = rate_ref.shape[1]
    members = width // rates_ref.shape[1]
    halves, rows = [], []
    for part in range(count // LANES):
        row = seg_ref[pl.ds((count // LANES) * pos + part, 1), :].astype(F32)
        rows.append(row)
        halves.append(jnp.transpose(jnp.broadcast_to(row, (LANES, LANES))))
    col = jnp.concatenate(halves, axis=0)

    def seg_at(spot):
        at = jnp.maximum(spot, 0)
        return jnp.where(spot < 0, 0, ids_ref[at])

    first = pos * count
    last = seg_at(first - 1).astype(F32)
    second = seg_at(first - 2).astype(F32)
    end = seg_at(first + count - 1).astype(F32)
    token = iota((count, LANES), 0)
    one = jnp.where(token == 0, last, pltpu.roll(col, 1, 0))
    two = jnp.where(token == 0, second, jnp.where(token == 1, last, pltpu.roll(col, 2, 0)))
    col_ref[0] = flag(col == one)
    col_ref[1] = flag(col == two)
    col_ref[2] = flag(col == last)
    col_ref[3] = flag(col == end)
    start = iota((count, LANES), 0) // SUB
    lead = jnp.zeros((count, LANES), F32)
    for c in range(count // SUB):
        lead = jnp.where(start == c, seg_at(first + c * SUB - 1).astype(F32), lead)
    col_ref[4] = flag(col == lead)
    lane = iota((SUB, SET), 1)
    inner = lax.rem(lane, SUB)
    tall = iota((SUB, SET), 0)
    for c in range(count // SUB):
        row = rows[c * SUB // LANES]
        shift = (c * SUB) % LANES
        base = row if shift == 0 else pltpu.roll(row, LANES - shift, 1)
        base = jnp.where(iota((1, LANES), 1) < SUB, base, 0.0)
        base = base + pltpu.roll(base, SUB, 1)
        base = base + pltpu.roll(base, 2 * SUB, 1)
        base = jnp.concatenate([base] * (SET // LANES), axis=1)
        mine = jnp.concatenate([col[c * SUB : (c + 1) * SUB]] * (SET // LANES), axis=1)
        tri_ref[c * SUB : (c + 1) * SUB, :] = flag((tall >= inner) & (mine == base)).astype(BF)
        keep_ref[c * 16 : (c + 1) * 16, :] = jnp.broadcast_to(
            flag(base == ids_ref[first + (c + 1) * SUB - 1].astype(F32)), (16, SET)).astype(BF)
    rates = rates_ref[...]
    weight = res_ref[...] * jnp.sqrt(rates)
    per = LANES * members
    onehot = flag(iota((LANES, per), 0) == iota((LANES, per), 1) // members).astype(BF)
    pick = iota((modes, per), 0) == lax.rem(iota((modes, per), 1), modes)
    for block in range(width // per):
        at = slice(block * LANES, (block + 1) * LANES)
        to = slice(block * per, (block + 1) * per)
        rate, wide = spread_out([rates[:, at], weight[:, at]], onehot)
        rate_ref[:, to] = rate
        flat_ref[0:1, to] = jnp.sum(jnp.where(pick, rate, 0.0), axis=0, keepdims=True)
        flat_ref[1:2, to] = jnp.sum(jnp.where(pick, wide, 0.0), axis=0, keepdims=True)

    def decay(rate, low, high):
        alive = flag(seg_at(low * count - 1) == seg_at(high * count - 1))
        return jnp.exp(-rate * (count * (high - low)).astype(F32)) * alive

    core = lax.rem(pos, 2)
    chip = pos // 2
    upper_half = rate_ref[:, pl.ds(pl.multiple_of(core * (width // 2), LANES), width // 2)]
    half_ref[0] = decay(upper_half, 2 * chip + 1, 2 * chip + 2)
    for k in range(rounds):
        reach = 1 << k
        base = (chip // reach) * reach
        up = lax.rem(chip // reach, 2)
        mate = base + reach * (1 - 2 * up)
        upf = up.astype(F32)
        half_ref[1 + 3 * k] = upf * decay(upper_half, 2 * base, 2 * chip)
        half_ref[2 + 3 * k] = jnp.where(up == 1, 1.0, decay(upper_half, 2 * mate, 2 * mate + 2 * reach))
        half_ref[3 + 3 * k] = jnp.where(up == 1, decay(upper_half, 2 * base, 2 * base + 2 * reach), 1.0)
    rate = rate_ref[...]
    full_ref[0] = jnp.where(core == 0, 1.0, decay(rate, 2 * chip, 2 * chip + 1))
    full_ref[1] = decay(rate, jnp.zeros_like(pos), pos)


def first_kernel(k_ref, v_ref, sw_ref, flat_ref, col_ref, u_ref, sum_ref):
    count, wide = u_ref.shape
    modes = sum_ref.shape[0]
    members = SET // modes
    token = iota((count, LANES), 0)
    one = col_ref[0]
    two = col_ref[1]
    owner = iota((modes, LANES), 1) // members
    for half in range(wide // LANES):
        at = slice(half * LANES, (half + 1) * LANES)
        made = []
        for index, ref in ((1, k_ref), (2, v_ref)):
            x = ref[:, at].astype(F32)
            made.append(
                sw_ref[index, 0:1, at] * x
                + sw_ref[index, 1:2, at] * (one * pltpu.roll(x, 1, 0))
                + sw_ref[index, 2:3, at] * (two * pltpu.roll(x, 2, 0))
            )
        u = jnp.where(token < 2, 0.0, made[0] * made[1]).astype(BF)
        u_ref[:, at] = u
        rflat = flat_ref[0:1, at]
        fine = jnp.exp(-rflat * (SUB - 1.0 - iota((SUB, LANES), 0).astype(F32)))
        spans = count // SUB
        coarse = jnp.exp(-rflat * (SUB * (spans - 1.0 - iota((spans, LANES), 0).astype(F32))))
        decay = jnp.concatenate([coarse[a : a + 1] * fine for a in range(spans)], axis=0)
        decay = (decay * col_ref[3]).astype(BF)
        sums = lax.dot_general(decay, u, (((0,), (0,)), ((), ())), preferred_element_type=F32)
        total = jnp.zeros((modes, LANES), F32)
        for g in range(LANES // members):
            total = jnp.where(owner == g, sums[g * modes : (g + 1) * modes], total)
        sum_ref[:, at] = total


def head_kernel(count, pos_ref, ids_ref, feat_ref, halo_ref, early_ref, sw_ref, rate_ref, sum_ref,
                total_ref, head_ref, use_ref):
    pos = pos_ref[0]
    width = rate_ref.shape[1]

    def seg_at(spot):
        at = jnp.maximum(spot, 0)
        return jnp.where(spot < 0, 0, ids_ref[at])

    first = pos * count
    s0, s1 = seg_at(first), seg_at(first + 1)
    end = seg_at(first + count - 1)
    p1, p2 = seg_at(first - 1), seg_at(first - 2)
    same = lambda a, b: (a == b).astype(F32)
    made = []
    for index in (0, 1, 2):
        h = jnp.where(pos == 0, early_ref[index].astype(F32), halo_ref[index].astype(F32))
        if index == 0:
            use_ref[...] = h
            continue
        x = feat_ref[index].astype(F32)
        x0, x1 = x[0:1], x[1:2]
        h2, h1 = h[0:1], h[1:2]
        w = [sw_ref[index, j : j + 1, :] for j in range(3)]
        f0 = w[0] * x0 + w[1] * (same(p1, s0) * h1) + w[2] * (same(p2, s0) * h2)
        f1 = w[0] * x1 + w[1] * (same(s0, s1) * x0) + w[2] * (same(p1, s1) * h1)
        made.append((f0, f1))
    u0 = (made[0][0] * made[1][0]).astype(BF).astype(F32)
    u1 = (made[0][1] * made[1][1]).astype(BF).astype(F32)
    head_ref[0:1, :] = u0
    head_ref[1:2, :] = u1
    half = width // 2
    for part in range(2):
        at = slice(part * half, (part + 1) * half)
        rate = rate_ref[:, at]
        total = sum_ref[:, at]
        total = total + jnp.exp(-rate * (count - 1.0)) * (same(s0, end) * u0[:, at])
        total = total + jnp.exp(-rate * (count - 2.0)) * (same(s1, end) * u1[:, at])
        total_ref[part] = total.astype(BF)


def local_kernel(piece, u_ref, head_ref, q_ref, halo_ref, sw_ref, skip_ref, rates_ref, res_ref, rate_ref, flat_ref,
                 col_ref, tri_ref, keep_ref, out_ref, gate_ref, cross_ref):
    count, wide = u_ref.shape
    modes = rates_ref.shape[0]
    members = 16
    groups = LANES // members
    spans = count // SUB
    at0 = (piece * (wide // members)) % LANES
    cols = wide // members * SUB
    lane = iota((1, cols), 1)
    rates = rates_ref[...]
    weight = res_ref[...] * jnp.sqrt(rates)
    filt = lane // SUB
    onehot = flag(iota((LANES, cols), 0) == filt + at0).astype(BF)
    (rate_to_end,) = spread_out([rates], onehot)
    decays = jnp.exp(-rate_to_end * (SUB - 1.0 - lax.rem(lane, SUB).astype(F32))).astype(BF)
    spot = lax.rem(lane, LANES)
    within = lax.rem((spot + SUB - 1) // SUB, LANES // SUB)
    lag = jnp.where(spot == 0, 0, lax.rem(SUB - lax.rem(spot, SUB), SUB)).astype(F32)
    filt = (lane // LANES) * (LANES // SUB) + within
    onehot = flag(iota((LANES, cols), 0) == filt + at0).astype(BF)
    rate_tap, weight_tap = spread_out([rates, weight], onehot)
    taps = jnp.sum(weight_tap * jnp.exp(-rate_tap * lag), axis=0, keepdims=True)

    token = iota((count, LANES), 0)
    owns = flag(iota((groups * SUB, LANES), 0) // SUB == iota((groups * SUB, LANES), 1) // members).astype(BF)
    holds = flag(iota((groups * modes, LANES), 0) // modes == iota((groups * modes, LANES), 1) // members).astype(BF)
    for tile in range(wide // LANES):
        at = slice(tile * LANES, (tile + 1) * LANES)
        u = u_ref[:, at].astype(F32)
        u = jnp.where(token == 0, head_ref[0:1, at], jnp.where(token == 1, head_ref[1:2, at], u))
        ub = u.astype(BF)
        rflat, wflat = flat_ref[0:1, at], flat_ref[1:2, at]
        near = []
        for part in range(SET // LANES):
            row = taps[:, tile * SET + part * LANES : tile * SET + (part + 1) * LANES]
            near.append(pltpu.roll(jnp.broadcast_to(row, (SUB, LANES)), 0, 1, stride=1, stride_axis=0))
        near = jnp.concatenate(near, axis=1).astype(BF)
        ends = decays[:, tile * SET : (tile + 1) * SET]
        table = wflat * jnp.exp(-rflat * (iota((SUB, LANES), 0).astype(F32) + 1.0))
        fall = jnp.exp(-rate_ref[:, at] * float(SUB))
        far = jnp.exp(-rflat * (SUB * iota((spans, LANES), 0).astype(F32)))
        inner, sums = [], []
        for c in range(spans):
            rows = slice(c * SUB, (c + 1) * SUB)
            left = jnp.concatenate([near * tri_ref[rows], ends * keep_ref[c * 16 : (c + 1) * 16]], axis=0)
            right = jnp.concatenate([ub[rows]] * groups, axis=0) * owns
            got = jnp.dot(left, right, preferred_element_type=F32)
            inner.append(got[:SUB])
            sums.append(got[SUB:])
            cross_ref[rows, at] = (table * far[c : c + 1] * col_ref[2, rows]).astype(BF)
        state = sums[0]
        local = [inner[0]]
        for c in range(1, spans):
            rows = slice(c * SUB, (c + 1) * SUB)
            seg_ok = flag_rows(col_ref, c)
            right = jnp.concatenate([state.astype(BF)] * groups, axis=0) * holds
            local.append(inner[c] + jnp.dot((table * seg_ok[0]).astype(BF), right, preferred_element_type=F32))
            state = fall * seg_ok[1] * state + sums[c]
        x = q_ref[:, at].astype(F32)
        h = halo_ref[:, at]
        one = jnp.where(token == 0, h[1:2], pltpu.roll(x, 1, 0))
        two = jnp.where(token == 0, h[0:1], jnp.where(token == 1, h[1:2], pltpu.roll(x, 2, 0)))
        q = sw_ref[0:1, at] * x + sw_ref[1:2, at] * (col_ref[0] * one) + sw_ref[2:3, at] * (col_ref[1] * two)
        gate_ref[:, at] = q
        out_ref[:, at] = q * (jnp.concatenate(local, axis=0) + skip_ref[:, at] * u)


def flag_rows(col_ref, c):
    rows = slice(c * SUB, (c + 1) * SUB)
    reach = col_ref[4, rows]
    return reach, reach[SUB - 1 : SUB]


def last_kernel(state_ref, table_ref, gate_ref, part_ref, out_ref):
    modes, wide = state_ref.shape
    members = 16
    groups = SET // members
    owner = iota((modes, SET), 1) // members
    for half in range(wide // SET):
        at = slice(half * SET, (half + 1) * SET)
        state = state_ref[:, at]
        spread = jnp.concatenate([jnp.where(owner == g, state, 0.0).astype(BF) for g in range(groups)], axis=0)
        cross = jnp.dot(table_ref[:, at], spread, preferred_element_type=F32)
        out_ref[:, at] = (part_ref[:, at] + gate_ref[:, at] * cross).astype(BF)


def params(limit=16 << 20):
    return pltpu.CompilerParams(vmem_limit_bytes=limit)


def fixed(shape):
    return pl.BlockSpec(shape, lambda i: (0,) * len(shape))


def lanes(rows, size, offset=0):
    return pl.BlockSpec((rows, size), lambda i: (0, offset + i))


def body(features, short_weight, residues, rates, skip, carry_state, earlier_rows, segment_ids):
    count, _, width = features.shape
    groups, modes = rates.shape
    blocks = lax.axis_size("ctx")
    pos = lax.axis_index("ctx")
    pos1 = pos.reshape(1)
    chips = blocks // 2
    rounds = chips.bit_length() - 1
    assert blocks == 2 << rounds and count == 2 * LANES and width == 16 * groups and modes == 16
    feat = jnp.transpose(features, (1, 0, 2))
    taps = jnp.transpose(short_weight, (1, 0, 2))
    early = jnp.transpose(earlier_rows, (1, 0, 2))
    segs = segment_ids.reshape(-1, LANES)
    rates_t = rates.T
    res_t = residues.T
    skip = skip.reshape(1, width)
    vm = pl.BlockSpec(memory_space=pltpu.VMEM)
    sm = pl.BlockSpec(memory_space=pltpu.SMEM)
    out = lambda *shape, dtype=F32: jax.ShapeDtypeStruct(shape, dtype)

    halo = lax.ppermute(feat[:, count - 2 :], "ctx", [(i, i + 1) for i in range(blocks - 1)])

    rate, flat, cols, tris, keeps, halves, fulls = pl.pallas_call(
        lambda *refs: plan_kernel(count, rounds, *refs),
        in_specs=[sm, vm, sm, vm, vm],
        out_specs=[vm] * 7,
        out_shape=[
            out(modes, width), out(2, width), out(5, count, LANES), out(count, SET, dtype=BF),
            out(count // SUB * 16, SET, dtype=BF), out(1 + 3 * rounds, modes, width // 2), out(2, modes, width),
        ],
        compiler_params=params(),
        name="plan",
    )(pos1, segs, segment_ids, rates_t, res_t)

    u, sums = pl.pallas_call(
        first_kernel,
        grid=(width // WIDE,),
        in_specs=[
            pl.BlockSpec((None, count, WIDE), lambda i: (1, 0, i)),
            pl.BlockSpec((None, count, WIDE), lambda i: (2, 0, i)),
            pl.BlockSpec((3, 3, WIDE), lambda i: (0, 0, i)),
            lanes(2, WIDE),
            fixed((5, count, LANES)),
        ],
        out_specs=[lanes(count, WIDE), lanes(modes, WIDE)],
        out_shape=[out(count, width, dtype=BF), out(modes, width)],
        compiler_params=params(),
        name="first",
    )(feat, feat, taps, flat, cols)

    total, head, halo_q = pl.pallas_call(
        lambda *refs: head_kernel(count, *refs),
        in_specs=[sm, sm] + [vm] * 6,
        out_specs=[vm] * 3,
        out_shape=[out(2, modes, width // 2, dtype=BF), out(2, width), out(2, width)],
        compiler_params=params(),
        name="head",
    )(pos1, segment_ids, feat[:, :2], halo, early, taps, rate, sums)

    pieces = width // WIDE
    parts = []
    for piece in range(pieces):
        mine = lambda rows, piece=piece: pl.BlockSpec((rows, WIDE), lambda i: (0, piece))
        group_block = piece * (WIDE // 16) // LANES
        few = pl.BlockSpec((modes, LANES), lambda i, b=group_block: (0, b))
        parts.append(pl.pallas_call(
            lambda *refs, piece=piece: local_kernel(piece, *refs),
            grid=(1,),
            in_specs=[
                mine(count), mine(2),
                pl.BlockSpec((None, count, WIDE), lambda i, piece=piece: (0, 0, piece)),
                mine(2),
                pl.BlockSpec((None, 3, WIDE), lambda i, piece=piece: (0, 0, piece)),
                mine(1), few, few, mine(modes), mine(2),
                fixed((5, count, LANES)), fixed((count, SET)), fixed((count // SUB * 16, SET)),
            ],
            out_specs=[lanes(count, WIDE)] * 3,
            out_shape=[out(count, WIDE), out(count, WIDE), out(count, WIDE, dtype=BF)],
            compiler_params=params(),
            cost_estimate=pl.CostEstimate(flops=4 << 30, bytes_accessed=5 << 20, transcendentals=0),
            name="local",
        )(u, head, feat, halo_q, taps, skip, rates_t, res_t, rate, flat, cols, tris, keeps))

    even = (pos & 1) == 0
    swap = lambda value: lax.ppermute(value, "ctx", [(i, i ^ 1) for i in range(blocks)])
    other = swap(total)
    low_total = jnp.where(even, total, other)
    own_half = lambda value: jnp.where(even, value[0], value[1]).astype(F32)
    chip_total = halves[0] * own_half(low_total) + own_half(jnp.where(even, other, total))
    before = jnp.zeros_like(chip_total)
    for k in range(rounds):
        got = lax.ppermute(chip_total.astype(BF), "ctx", [(i, i ^ (2 << k)) for i in range(blocks)]).astype(F32)
        before = before + halves[1 + 3 * k] * got
        chip_total = halves[2 + 3 * k] * chip_total + halves[3 + 3 * k] * got
    mine = before.astype(BF)
    yours = swap(mine)
    full = jnp.concatenate([jnp.where(even, mine, yours), jnp.where(even, yours, mine)], axis=1).astype(F32)
    low_full = jnp.where(even, 0.0, jnp.concatenate([low_total[0], low_total[1]], axis=1).astype(F32))
    state = fulls[0] * full + low_full + fulls[1] * carry_state

    done = []
    for piece in range(pieces):
        part, gate, table = parts[piece]
        done.append(pl.pallas_call(
            last_kernel,
            grid=(1,),
            in_specs=[pl.BlockSpec((modes, WIDE), lambda i, piece=piece: (0, piece))] + [lanes(count, WIDE)] * 3,
            out_specs=lanes(count, WIDE),
            out_shape=out(count, WIDE, dtype=BF),
            compiler_params=params(),
            name="last",
        )(state, table, gate, part))
    return jnp.concatenate(done, axis=1)


def solution(mesh):
    placed = (
        P(("groups", "ctx"), None, None),
        P(),
        P(),
        P(),
        P(),
        P("groups", None),
        P("groups", None, None),
        P("groups"),
    )
    return jax.shard_map(
        body, mesh=mesh, in_specs=placed, out_specs=P(("groups", "ctx"), None), check_vma=False
    )
```

```python
import jax
import jax.numpy as jnp
from jax import lax
from jax.experimental import pallas as pl
from jax.experimental.pallas import tpu as pltpu
from jax.sharding import PartitionSpec as P

BF = jnp.bfloat16
F32 = jnp.float32
LANES = 128
SET = 256
WIDE = 1024
SUB = 32


def iota(shape, dim):
    return lax.broadcasted_iota(jnp.int32, shape, dim)


def flag(x):
    return x.astype(F32)


def split3(x):
    hi = x.astype(BF)
    rest = x - hi.astype(F32)
    mid = rest.astype(BF)
    low = (rest - mid.astype(F32)).astype(BF)
    return [hi, mid, low]


def spread_out(values, onehot):
    rows = values[0].shape[0]
    pieces = sum([split3(value) for value in values], [])
    got = jnp.dot(jnp.concatenate(pieces, axis=0), onehot, preferred_element_type=F32)
    part = lambda i: got[i * rows : (i + 1) * rows]
    return [(part(3 * i) + part(3 * i + 1)) + part(3 * i + 2) for i in range(len(values))]


def first_kernel(pos_ref, seg_hbm, rates_hbm, feat_ref, taps_hbm,
                 u_ref, q_ref, sum_ref, rate_ref, flat_ref, edge_ref, col_ref, shift_ref, taps_ref,
                 keep_ref, kv_ref, seg_ref, rates_ref, sems):
    pos = pos_ref[0]
    count, width = u_ref.shape
    modes = sum_ref.shape[0]
    members = SET // modes
    chunks = width // WIDE

    def copies(chunk):
        at = slice(chunk * WIDE, (chunk + 1) * WIDE)
        return [
            pltpu.make_async_copy(feat_ref.at[1 + i, :, at], kv_ref.at[i, :, at], sems.at[2 * chunk + i])
            for i in range(2)
        ]

    small = [
        pltpu.make_async_copy(source, target, sems.at[2 * chunks + i])
        for i, (source, target) in enumerate(((seg_hbm, seg_ref), (rates_hbm, rates_ref), (taps_hbm, taps_ref)))
    ]
    q_copy = pltpu.make_async_copy(feat_ref.at[0], q_ref, sems.at[2 * chunks + 3])
    for copy in small:
        copy.start()
    for chunk in range(chunks):
        for copy in copies(chunk):
            copy.start()
    q_copy.start()
    for copy in small:
        copy.wait()

    @pl.when(pos >= 0)
    def _():
        token = iota((count, LANES), 0)
        halves, rows = [], []
        for part in range(count // LANES):
            row = seg_ref[pl.ds((count // LANES) * pos + part, 1), :].astype(F32)
            rows.append(row)
            halves.append(jnp.transpose(jnp.broadcast_to(row, (LANES, LANES))))
        col = jnp.concatenate(halves, axis=0)
        before = seg_ref[pl.ds(jnp.maximum((count // LANES) * pos - 1, 0), 1), :].astype(F32)
        before = jnp.where(pos == 0, 0.0, before)
        last = jnp.broadcast_to(before[:, LANES - 1 :], (1, LANES))
        end = jnp.broadcast_to(rows[-1][:, LANES - 1 :], (1, LANES))
        col_ref[0] = flag(col == last)
        col_ref[1] = col
        keep_ref[...] = flag((col == end) & (token >= 2)).astype(BF)
        every = jnp.concatenate(rows, axis=1)
        there = jnp.concatenate([col] * (count // LANES), axis=1)
        gap = iota((count, count), 0) - iota((count, count), 1)
        for step in (1, 2):
            shift_ref[(step - 1) * count : step * count, :] = flag((gap == step) & (there == every)).astype(BF)

        per = LANES * members
        onehot = flag(iota((LANES, per), 0) == iota((LANES, per), 1) // members).astype(BF)
        pick = iota((modes, per), 0) == lax.rem(iota((modes, per), 1), modes)
        for block in range(width // per):
            at = slice(block * LANES, (block + 1) * LANES)
            to = slice(block * per, (block + 1) * per)
            (rate,) = spread_out([rates_ref[:, at]], onehot)
            rate_ref[:, to] = rate
            flat_ref[:, to] = jnp.sum(jnp.where(pick, rate, 0.0), axis=0, keepdims=True)

    owner = iota((modes, LANES), 1) // members
    spans = count // SUB

    def two_tiles(start):
        both = pl.ds(start, SET)
        shifted = []
        for index in (1, 2):
            edge_ref[2 * index - 2 : 2 * index, both] = kv_ref[index - 1, :16, both].astype(F32)[:2]
            shifted.append(jnp.dot(shift_ref[...], kv_ref[index - 1, :, both], preferred_element_type=F32))
        for part in range(SET // LANES):
            at = pl.ds(start + part * LANES, LANES)
            cut = slice(part * LANES, (part + 1) * LANES)
            made = []
            for index in (1, 2):
                moved = shifted[index - 1]
                made.append(
                    taps_ref[0, index : index + 1, at] * kv_ref[index - 1, :, at].astype(F32)
                    + taps_ref[1, index : index + 1, at] * moved[:count, cut]
                    + taps_ref[2, index : index + 1, at] * moved[count:, cut]
                )
            u = (made[0] * made[1]).astype(BF)
            u_ref[:, at] = u

    def sums_of(start):
        at = pl.ds(start, SET)
        rflat = flat_ref[:, at]
        fine = jnp.exp(-rflat * (SUB - 1.0 - iota((SUB, SET), 0).astype(F32)))
        coarse = jnp.exp(-rflat * (SUB * (spans - 1.0 - iota((spans, SET), 0).astype(F32))))
        decay = jnp.concatenate([(coarse[a : a + 1] * fine).astype(BF) for a in range(spans)], axis=0)
        decay = decay * jnp.concatenate([keep_ref[...]] * (SET // LANES), axis=1)
        sums = lax.dot_general(decay, u_ref[:, at], (((0,), (0,)), ((), ())), preferred_element_type=F32)
        for part in range(SET // LANES):
            cut = slice(part * LANES, (part + 1) * LANES)
            total = jnp.zeros((modes, LANES), F32)
            for g in range(LANES // members):
                row = part * LANES + g * modes
                total = jnp.where(owner == g, sums[row : row + modes, cut], total)
            sum_ref[:, pl.ds(start + part * LANES, LANES)] = total

    for chunk in range(chunks):
        for copy in copies(chunk):
            copy.wait()

        @pl.when(pos >= 0)
        def _():
            for i in range(WIDE // SET):
                two_tiles(chunk * WIDE + i * SET)

    @pl.when(pos >= 0)
    def _():
        for i in range(width // SET):
            sums_of(i * SET)

    q_copy.wait()


def head_kernel(count, pos_ref, seg_ref, edge_ref, halo_ref, early_ref, sw_ref, rate_ref, sum_ref, u_ref, q_ref,
                total_ref, head_ref, use_ref):
    pos = pos_ref[0]
    width = rate_ref.shape[1]
    per = count // LANES
    row = seg_ref[pl.ds(per * pos, 1), :]
    tail = seg_ref[pl.ds(per * pos + per - 1, 1), :]
    before = seg_ref[pl.ds(jnp.maximum(per * pos - 1, 0), 1), :]
    before = jnp.where(pos == 0, 0, before)
    s0, s1 = row[:, 0:1], row[:, 1:2]
    end = tail[:, LANES - 1 :]
    p1, p2 = before[:, LANES - 1 :], before[:, LANES - 2 : LANES - 1]
    same = lambda a, b: jnp.broadcast_to(flag(a == b), (1, width))
    near, far = same(p1, s0), same(p2, s0)
    step, skip = same(s0, s1), same(p1, s1)
    made = []
    for index in (0, 1, 2):
        h = jnp.where(pos == 0, early_ref[index].astype(F32), halo_ref[index].astype(F32))
        h2, h1 = h[0:1], h[1:2]
        w = [sw_ref[j, index : index + 1, :] for j in range(3)]
        if index == 0:
            use_ref[0:1, :] = w[1] * (near * h1) + w[2] * (far * h2)
            use_ref[1:2, :] = w[2] * (skip * h1)
            continue
        x0, x1 = edge_ref[2 * index - 2 : 2 * index - 1], edge_ref[2 * index - 1 : 2 * index]
        f0 = w[0] * x0 + w[1] * (near * h1) + w[2] * (far * h2)
        f1 = w[0] * x1 + w[1] * (step * x0) + w[2] * (skip * h1)
        made.append((f0, f1))
    u0 = (made[0][0] * made[1][0]).astype(BF).astype(F32)
    u1 = (made[0][1] * made[1][1]).astype(BF).astype(F32)
    head_ref[0:1, :] = u0
    head_ref[1:2, :] = u1
    u0 = same(s0, end) * u0
    u1 = same(s1, end) * u1
    half = width // 2
    for part in range(2):
        at = slice(part * half, (part + 1) * half)
        rate = rate_ref[:, at]
        drop = jnp.exp(-rate * (count - 2.0))
        total_ref[part] = (sum_ref[:, at] + drop * (u1[:, at] + jnp.exp(-rate) * u0[:, at])).astype(BF)


def plan_kernel(count, rounds, pos_ref, seg_ref, ids_ref, rates_ref, res_ref, rate_ref, col_ref, u_ref, q_ref,
                wide_ref, lead_ref, tri_ref, keep_ref, half_ref, full_ref):
    pos = pos_ref[0]
    modes = rates_ref.shape[0]
    width = rate_ref.shape[1]
    members = width // rates_ref.shape[1]

    def seg_at(spot):
        at = jnp.maximum(spot, 0)
        return jnp.where(spot < 0, 0, ids_ref[at])

    first = pos * count
    col = col_ref[1]
    start = iota((count, LANES), 0) // SUB
    lead = jnp.zeros((count, LANES), F32)
    for c in range(count // SUB):
        lead = jnp.where(start == c, seg_at(first + c * SUB - 1).astype(F32), lead)
    lead_ref[...] = flag(col == lead)
    inner = lax.rem(iota((SUB, SET), 1), SUB)
    tall = iota((SUB, SET), 0)
    for c in range(count // SUB):
        row = seg_ref[pl.ds((count // LANES) * pos + c * SUB // LANES, 1), :].astype(F32)
        shift = (c * SUB) % LANES
        base = row if shift == 0 else pltpu.roll(row, LANES - shift, 1)
        base = jnp.where(iota((1, LANES), 1) < SUB, base, 0.0)
        base = base + pltpu.roll(base, SUB, 1)
        base = base + pltpu.roll(base, 2 * SUB, 1)
        base = jnp.concatenate([base] * (SET // LANES), axis=1)
        mine = jnp.concatenate([col[c * SUB : (c + 1) * SUB]] * (SET // LANES), axis=1)
        tri_ref[c * SUB : (c + 1) * SUB, :] = flag((tall >= inner) & (mine == base)).astype(BF)
        keep_ref[c * modes : (c + 1) * modes, :] = jnp.broadcast_to(
            flag(base == ids_ref[first + (c + 1) * SUB - 1].astype(F32)), (modes, SET)).astype(BF)
    weight = res_ref[...] * jnp.sqrt(rates_ref[...])
    per = LANES * members
    onehot = flag(iota((LANES, per), 0) == iota((LANES, per), 1) // members).astype(BF)
    pick = iota((modes, per), 0) == lax.rem(iota((modes, per), 1), modes)
    for block in range(width // per):
        at = slice(block * LANES, (block + 1) * LANES)
        to = slice(block * per, (block + 1) * per)
        (spread,) = spread_out([weight[:, at]], onehot)
        wide_ref[:, to] = jnp.sum(jnp.where(pick, spread, 0.0), axis=0, keepdims=True)

    def decay(rate, low, high):
        alive = flag(seg_at(low * count - 1) == seg_at(high * count - 1))
        return jnp.exp(-rate * (count * (high - low)).astype(F32)) * alive

    core = lax.rem(pos, 2)
    chip = pos // 2
    rate = rate_ref[:, pl.ds(pl.multiple_of(core * (width // 2), LANES), width // 2)]
    half_ref[0] = decay(rate, 2 * chip + 1, 2 * chip + 2)
    spot = 1
    reach = 1
    for radix in rounds:
        size = reach * radix
        top = 2 * (chip // size) * size + 2 * size
        own = 2 * (chip // reach) * reach + 2 * reach
        half_ref[spot] = decay(rate, own, top)
        for other in range(1, radix):
            group = (chip // reach) ^ other
            finish = 2 * (group + 1) * reach
            ahead = group < chip // reach
            half_ref[spot + 1] = flag(ahead) * decay(rate, jnp.where(ahead, finish, 0), 2 * chip)
            half_ref[spot + 2] = decay(rate, finish, top)
            spot += 2
        spot += 1
        reach = size
    rate = rate_ref[...]
    full_ref[0] = jnp.where(core == 0, 1.0, decay(rate, 2 * chip, 2 * chip + 1))
    full_ref[1] = decay(rate, jnp.zeros_like(pos), pos)


def local_kernel(base, u_ref, head_ref, q_ref, halo_ref, sw_ref, skip_ref, rates_ref, res_ref, rate_ref, flat_ref,
                 wide_ref, lead_ref, col_ref, shift_ref, tri_ref, keep_ref, out_ref, gate_ref, cross_ref):
    count, wide = out_ref.shape
    modes = rates_ref.shape[0]
    members = 16
    groups = LANES // members
    spans = count // SUB
    first = base // members
    block = slice(first // LANES * LANES, first // LANES * LANES + LANES)
    cols = wide // members * SUB
    lane = iota((1, cols), 1)
    rates = rates_ref[:, block]
    weight = res_ref[:, block] * jnp.sqrt(rates)
    filt = lane // SUB + first % LANES
    onehot = flag(iota((LANES, cols), 0) == filt).astype(BF)
    (rate_to_end,) = spread_out([rates], onehot)
    decays = jnp.exp(-rate_to_end * (SUB - 1.0 - lax.rem(lane, SUB).astype(F32))).astype(BF)
    spot = lax.rem(lane, LANES)
    within = lax.rem((spot + SUB - 1) // SUB, LANES // SUB)
    lag = jnp.where(spot == 0, 0, lax.rem(SUB - lax.rem(spot, SUB), SUB)).astype(F32)
    filt = (lane // LANES) * (LANES // SUB) + within + first % LANES
    onehot = flag(iota((LANES, cols), 0) == filt).astype(BF)
    rate_tap, weight_tap = spread_out([rates, weight], onehot)
    taps = jnp.sum(weight_tap * jnp.exp(-rate_tap * lag), axis=0, keepdims=True)

    token = iota((16, LANES), 0)
    pad = lambda x, rows: jnp.concatenate([x, jnp.zeros((rows - x.shape[0], x.shape[1]), F32)], axis=0)
    owns = flag(iota((groups * SUB, LANES), 0) // SUB == iota((groups * SUB, LANES), 1) // members).astype(BF)
    holds = flag(iota((groups * modes, LANES), 0) // modes == iota((groups * modes, LANES), 1) // members).astype(BF)
    for tile in range(wide // LANES):
        at = slice(tile * LANES, (tile + 1) * LANES)
        to = slice(base + tile * LANES, base + (tile + 1) * LANES)
        ub = u_ref[:, to]
        start = jnp.where(token < 2, pad(head_ref[:, to], 16), ub[:16].astype(F32)).astype(BF)
        ub = jnp.concatenate([start, ub[16:]], axis=0)
        rflat, wflat = flat_ref[:, to], wide_ref[:, to]
        near = []
        for part in range(SET // LANES):
            row = taps[:, tile * SET + part * LANES : tile * SET + (part + 1) * LANES]
            near.append(pltpu.roll(jnp.broadcast_to(row, (SUB, LANES)), 0, 1, stride=1, stride_axis=0))
        near = jnp.concatenate(near, axis=1).astype(BF)
        ends = decays[:, tile * SET : (tile + 1) * SET]
        table = wflat * jnp.exp(-rflat * (iota((SUB, LANES), 0).astype(F32) + 1.0))
        fall = jnp.exp(-rate_ref[:, to] * float(SUB))
        far = jnp.exp(-rflat * (SUB * iota((spans, LANES), 0).astype(F32)))
        inner, sums = [], []
        for c in range(spans):
            rows = slice(c * SUB, (c + 1) * SUB)
            left = jnp.concatenate([near * tri_ref[rows], ends * keep_ref[c * 16 : (c + 1) * 16]], axis=0)
            right = jnp.concatenate([ub[rows]] * groups, axis=0) * owns
            got = jnp.dot(left, right, preferred_element_type=F32)
            inner.append(got[:SUB])
            sums.append(got[SUB:])
            cross_ref[rows, at] = (table * far[c : c + 1] * col_ref[0, rows]).astype(BF)
        state = sums[0]
        local = [inner[0]]
        for c in range(1, spans):
            rows = slice(c * SUB, (c + 1) * SUB)
            reach = lead_ref[rows]
            right = jnp.concatenate([state.astype(BF)] * groups, axis=0) * holds
            local.append(inner[c] + jnp.dot((table * reach).astype(BF), right, preferred_element_type=F32))
            state = fall * reach[SUB - 1 :] * state + sums[c]
        out_ref[:, at] = jnp.concatenate(local, axis=0) + skip_ref[:, to] * ub.astype(F32)
    for part in range(wide // SET):
        at = slice(part * SET, (part + 1) * SET)
        to = slice(base + part * SET, base + (part + 1) * SET)
        moved = jnp.dot(shift_ref[...], q_ref[:, to], preferred_element_type=F32)
        q = (
            sw_ref[0, 0:1, to] * q_ref[:, to].astype(F32)
            + sw_ref[1, 0:1, to] * moved[:count]
            + sw_ref[2, 0:1, to] * moved[count:]
        )
        q = jnp.concatenate([q[:8] + pad(halo_ref[:, to], 8), q[8:]], axis=0)
        gate_ref[:, at] = q
        out_ref[:, at] = q * out_ref[:, at]


def last_kernel(pieces, state_ref, *refs):
    modes = state_ref.shape[0]
    members = 16
    groups = SET // members
    owner = iota((modes, SET), 1) // members
    out_ref, made_ref, sems = refs[3 * pieces :]
    copies = []
    for piece in range(pieces):
        part_ref, gate_ref, table_ref = refs[3 * piece : 3 * piece + 3]
        wide = part_ref.shape[1]
        for half in range(wide // SET):
            at = slice(half * SET, (half + 1) * SET)
            to = slice(piece * wide + half * SET, piece * wide + (half + 1) * SET)
            state = state_ref[:, to]
            spread = jnp.concatenate([jnp.where(owner == g, state, 0.0).astype(BF) for g in range(groups)], axis=0)
            cross = jnp.dot(table_ref[:, at], spread, preferred_element_type=F32)
            made_ref[:, to] = (part_ref[:, at] + gate_ref[:, at] * cross).astype(BF)
        to = slice(piece * wide, (piece + 1) * wide)
        copies.append(pltpu.make_async_copy(made_ref.at[:, to], out_ref.at[:, to], sems.at[piece]))
        copies[-1].start()
    for copy in copies:
        copy.wait()


def params(limit=16 << 20):
    return pltpu.CompilerParams(vmem_limit_bytes=limit)


def body(features, short_weight, residues, rates, skip, carry_state, earlier_rows, segment_ids):
    count, _, width = features.shape
    groups, modes = rates.shape
    blocks = lax.axis_size("ctx")
    pos = lax.axis_index("ctx")
    pos1 = pos.reshape(1)
    chips = blocks // 2
    bits = chips.bit_length() - 1
    rounds = ([4] if bits > 1 else []) + [2] * (bits - 2 if bits > 1 else bits)
    assert blocks == 2 << bits and count == 2 * LANES and width == 16 * groups and modes == 16
    feat = jnp.transpose(features, (1, 0, 2))
    early = jnp.transpose(earlier_rows, (1, 0, 2))
    segs = segment_ids.reshape(-1, LANES)
    rates_t = rates.T
    res_t = residues.T
    skip = skip.reshape(1, width)
    vm = pl.BlockSpec(memory_space=pltpu.VMEM)
    sm = pl.BlockSpec(memory_space=pltpu.SMEM)
    out = lambda *shape, dtype=F32: jax.ShapeDtypeStruct(shape, dtype)
    stay = lambda value: pltpu.with_memory_space_constraint(value, pltpu.HBM)
    swap = lambda value, by: lax.ppermute(value, "ctx", [(i, i ^ by) for i in range(blocks)])
    tie = lambda *values: lax.optimization_barrier(values)

    halo = lax.ppermute(feat[:, count - 2 :], "ctx", [(i, i + 1) for i in range(blocks - 1)])

    hbm = pl.BlockSpec(memory_space=pltpu.HBM)
    u, q, sums, rate, flat, edge, cols, shifts, weights = pl.pallas_call(
        first_kernel,
        in_specs=[sm, hbm, hbm, hbm, hbm],
        out_specs=[vm] * 9,
        out_shape=[out(count, width, dtype=BF), out(count, width, dtype=BF), out(modes, width), out(modes, width),
                   out(1, width), out(4, width), out(2, count, LANES), out(2 * count, count, dtype=BF),
                   out(*short_weight.shape)],
        scratch_shapes=[
            pltpu.VMEM((count, LANES), BF), pltpu.VMEM((2, count, width), BF), pltpu.VMEM(segs.shape, jnp.int32),
            pltpu.VMEM(rates_t.shape, F32), pltpu.SemaphoreType.DMA((2 * (width // WIDE) + 4,)),
        ],
        compiler_params=params(),
        name="first",
    )(pos1, stay(segs), stay(rates_t), stay(feat), stay(short_weight))

    total, head, halo_q = pl.pallas_call(
        lambda *refs: head_kernel(count, *refs),
        in_specs=[sm] + [vm] * 9,
        out_specs=[vm] * 3,
        out_shape=[out(2, modes, width // 2, dtype=BF), out(2, width), out(2, width)],
        compiler_params=params(),
        name="head",
    )(pos1, segs, edge, halo, early, weights, rate, sums, u, q)

    even = (pos & 1) == 0
    other = swap(total, 1)
    steps = 1 + sum(2 * radix - 1 for radix in rounds)
    wflat, lead, tris, keeps, halves, fulls = pl.pallas_call(
        lambda *refs: plan_kernel(count, rounds, *refs),
        in_specs=[sm, vm, sm] + [vm] * 6,
        out_specs=[vm] * 6,
        out_shape=[
            out(1, width), out(count, LANES), out(count, SET, dtype=BF), out(count // SUB * 16, SET, dtype=BF),
            out(steps, modes, width // 2), out(2, modes, width),
        ],
        compiler_params=params(),
        cost_estimate=pl.CostEstimate(flops=1 << 30, bytes_accessed=5 << 20, transcendentals=0),
        name="plan",
    )(pos1, segs, segment_ids, rates_t, res_t, rate, cols, u, q)

    pieces = width // WIDE
    parts = []

    def local(piece, head):
        return pl.pallas_call(
            lambda *refs: local_kernel(piece * WIDE, *refs),
            in_specs=[vm] * 16,
            out_specs=[vm] * 3,
            out_shape=[out(count, WIDE), out(count, WIDE), out(count, WIDE, dtype=BF)],
            compiler_params=params(),
            cost_estimate=pl.CostEstimate(flops=4 << 30, bytes_accessed=5 << 20, transcendentals=0),
            name="local",
        )(u, head, q, halo_q, weights, skip, rates_t, res_t, rate, flat, wflat, lead, cols, shifts, tris, keeps)

    low_total = jnp.where(even, total, other)
    own_half = lambda value: jnp.where(even, value[0], value[1]).astype(F32)
    chip_total = halves[0] * own_half(low_total) + own_half(jnp.where(even, other, total))
    chip_total, head = tie(chip_total, head)
    before = jnp.zeros_like(chip_total)
    spot, reach = 1, 1
    left = list(range(pieces))
    for number, radix in enumerate(rounds):
        sent = chip_total.astype(BF)
        got = [swap(sent, 2 * reach * i).astype(F32) for i in range(1, radix)]
        share = -(-len(left) // (len(rounds) - number))
        for piece in left[:share]:
            parts.append(local(piece, head))
        left = left[share:]
        got, parts, head = tie(got, parts, head)
        chip_total = halves[spot] * chip_total
        for i in range(radix - 1):
            before = before + halves[spot + 1 + 2 * i] * got[i]
            chip_total = chip_total + halves[spot + 2 + 2 * i] * got[i]
        spot += 2 * radix - 1
        reach *= radix
    mine = before.astype(BF)
    yours = swap(mine, 1)
    full = jnp.concatenate([jnp.where(even, mine, yours), jnp.where(even, yours, mine)], axis=1).astype(F32)
    low_full = jnp.where(even, 0.0, jnp.concatenate([low_total[0], low_total[1]], axis=1).astype(F32))
    state = fulls[0] * full + low_full + fulls[1] * carry_state

    return pl.pallas_call(
        lambda *refs: last_kernel(pieces, *refs),
        in_specs=[vm] * (1 + 3 * pieces),
        out_specs=hbm,
        out_shape=out(count, width, dtype=BF),
        scratch_shapes=[pltpu.VMEM((count, width), BF), pltpu.SemaphoreType.DMA((pieces,))],
        compiler_params=params(),
        name="last",
    )(state, *[value for piece in parts for value in piece])


def solution(mesh):
    placed = (
        P(("groups", "ctx"), None, None),
        P(),
        P(),
        P(),
        P(),
        P("groups", None),
        P("groups", None, None),
        P("groups"),
    )
    return jax.shard_map(
        body, mesh=mesh, in_specs=placed, out_specs=P(("groups", "ctx"), None), check_vma=False
    )
```

```python
import jax
import jax.numpy as jnp
from jax import lax
from jax.experimental import pallas as pl
from jax.experimental.pallas import tpu as pltpu
from jax.sharding import PartitionSpec as P

BF = jnp.bfloat16
F32 = jnp.float32
LANES = 128
SET = 256
WIDE = 1024
SUB = 32


def iota(shape, dim):
    return lax.broadcasted_iota(jnp.int32, shape, dim)


def flag(x):
    return x.astype(F32)


def split3(x):
    hi = x.astype(BF)
    rest = x - hi.astype(F32)
    mid = rest.astype(BF)
    low = (rest - mid.astype(F32)).astype(BF)
    return [hi, mid, low]


def spread_out(values, onehot):
    rows = values[0].shape[0]
    pieces = sum([split3(value) for value in values], [])
    got = jnp.dot(jnp.concatenate(pieces, axis=0), onehot, preferred_element_type=F32)
    part = lambda i: got[i * rows : (i + 1) * rows]
    return [(part(3 * i) + part(3 * i + 1)) + part(3 * i + 2) for i in range(len(values))]


def first_kernel(pos_ref, seg_hbm, rates_hbm, feat_ref, taps_hbm,
                 u_ref, q_ref, sum_ref, rate_ref, flat_ref, edge_ref, col_ref, taps_ref,
                 keep_ref, shift_ref, kv_ref, seg_ref, rates_ref, sems):
    pos = pos_ref[0]
    count, width = u_ref.shape
    modes = sum_ref.shape[0]
    members = SET // modes
    chunks = width // WIDE

    def copies(chunk):
        at = slice(chunk * WIDE, (chunk + 1) * WIDE)
        return [
            pltpu.make_async_copy(feat_ref.at[1 + i, :, at], kv_ref.at[i, :, at], sems.at[2 * chunk + i])
            for i in range(2)
        ]

    small = [
        pltpu.make_async_copy(source, target, sems.at[2 * chunks + i])
        for i, (source, target) in enumerate(((seg_hbm, seg_ref), (rates_hbm, rates_ref), (taps_hbm, taps_ref)))
    ]
    q_copy = pltpu.make_async_copy(feat_ref.at[0], q_ref, sems.at[2 * chunks + 3])
    for copy in small:
        copy.start()
    for chunk in range(chunks):
        for copy in copies(chunk):
            copy.start()
    q_copy.start()
    for copy in small:
        copy.wait()

    @pl.when(pos >= 0)
    def _():
        token = iota((count, LANES), 0)
        halves, rows = [], []
        for part in range(count // LANES):
            row = seg_ref[pl.ds((count // LANES) * pos + part, 1), :].astype(F32)
            rows.append(row)
            halves.append(jnp.transpose(jnp.broadcast_to(row, (LANES, LANES))))
        col = jnp.concatenate(halves, axis=0)
        before = seg_ref[pl.ds(jnp.maximum((count // LANES) * pos - 1, 0), 1), :].astype(F32)
        before = jnp.where(pos == 0, 0.0, before)
        last = jnp.broadcast_to(before[:, LANES - 1 :], (1, LANES))
        end = jnp.broadcast_to(rows[-1][:, LANES - 1 :], (1, LANES))
        col_ref[0] = flag(col == last)
        col_ref[1] = col
        keep_ref[...] = flag((col == end) & (token >= 2)).astype(BF)
        col_ref[2] = flag((col == pltpu.roll(col, 1, 0)) & (token >= 1))
        col_ref[3] = flag((col == pltpu.roll(col, 2, 0)) & (token >= 2))
        every = jnp.concatenate(rows, axis=1)
        there = jnp.concatenate([col] * (count // LANES), axis=1)
        gap = iota((count, count), 0) - iota((count, count), 1)
        for step in (1, 2):
            shift_ref[(step - 1) * count : step * count, :] = flag((gap == step) & (there == every)).astype(BF)

        per = LANES * members
        onehot = flag(iota((LANES, per), 0) == iota((LANES, per), 1) // members).astype(BF)
        pick = iota((modes, per), 0) == lax.rem(iota((modes, per), 1), modes)
        for block in range(width // per):
            at = slice(block * LANES, (block + 1) * LANES)
            to = slice(block * per, (block + 1) * per)
            (rate,) = spread_out([rates_ref[:, at]], onehot)
            rate_ref[:, to] = rate
            flat_ref[:, to] = jnp.sum(jnp.where(pick, rate, 0.0), axis=0, keepdims=True)

    owner = iota((modes, LANES), 1) // members
    spans = count // SUB

    def two_tiles(start):
        both = pl.ds(start, SET)
        shifted = []
        for index in (1, 2):
            edge_ref[2 * index - 2 : 2 * index, both] = kv_ref[index - 1, :16, both].astype(F32)[:2]
            shifted.append(jnp.dot(shift_ref[...], kv_ref[index - 1, :, both], preferred_element_type=F32))
        for part in range(SET // LANES):
            at = pl.ds(start + part * LANES, LANES)
            cut = slice(part * LANES, (part + 1) * LANES)
            made = []
            for index in (1, 2):
                moved = shifted[index - 1]
                made.append(
                    taps_ref[0, index : index + 1, at] * kv_ref[index - 1, :, at].astype(F32)
                    + taps_ref[1, index : index + 1, at] * moved[:count, cut]
                    + taps_ref[2, index : index + 1, at] * moved[count:, cut]
                )
            u = (made[0] * made[1]).astype(BF)
            u_ref[:, at] = u

    def sums_of(start):
        at = pl.ds(start, SET)
        rflat = flat_ref[:, at]
        fine = jnp.exp(-rflat * (SUB - 1.0 - iota((SUB, SET), 0).astype(F32)))
        coarse = jnp.exp(-rflat * (SUB * (spans - 1.0 - iota((spans, SET), 0).astype(F32))))
        decay = jnp.concatenate([(coarse[a : a + 1] * fine).astype(BF) for a in range(spans)], axis=0)
        decay = decay * jnp.concatenate([keep_ref[...]] * (SET // LANES), axis=1)
        sums = lax.dot_general(decay, u_ref[:, at], (((0,), (0,)), ((), ())), preferred_element_type=F32)
        for part in range(SET // LANES):
            cut = slice(part * LANES, (part + 1) * LANES)
            total = jnp.zeros((modes, LANES), F32)
            for g in range(LANES // members):
                row = part * LANES + g * modes
                total = jnp.where(owner == g, sums[row : row + modes, cut], total)
            sum_ref[:, pl.ds(start + part * LANES, LANES)] = total

    for chunk in range(chunks):
        for copy in copies(chunk):
            copy.wait()

        @pl.when(pos >= 0)
        def _():
            for i in range(WIDE // SET):
                two_tiles(chunk * WIDE + i * SET)

    @pl.when(pos >= 0)
    def _():
        for i in range(width // SET):
            sums_of(i * SET)

    q_copy.wait()


def head_kernel(count, pos_ref, seg_ref, edge_ref, halo_ref, early_ref, sw_ref, rate_ref, sum_ref,
                total_ref, head_ref, use_ref):
    pos = pos_ref[0]
    width = rate_ref.shape[1]
    per = count // LANES
    row = seg_ref[pl.ds(per * pos, 1), :]
    tail = seg_ref[pl.ds(per * pos + per - 1, 1), :]
    before = seg_ref[pl.ds(jnp.maximum(per * pos - 1, 0), 1), :]
    before = jnp.where(pos == 0, 0, before)
    s0, s1 = row[:, 0:1], row[:, 1:2]
    end = tail[:, LANES - 1 :]
    p1, p2 = before[:, LANES - 1 :], before[:, LANES - 2 : LANES - 1]
    same = lambda a, b: jnp.broadcast_to(flag(a == b), (1, width))
    near, far = same(p1, s0), same(p2, s0)
    step, skip = same(s0, s1), same(p1, s1)
    made = []
    for index in (0, 1, 2):
        h = jnp.where(pos == 0, early_ref[index].astype(F32), halo_ref[index].astype(F32))
        h2, h1 = h[0:1], h[1:2]
        w = [sw_ref[j, index : index + 1, :] for j in range(3)]
        if index == 0:
            use_ref[0:1, :] = w[1] * (near * h1) + w[2] * (far * h2)
            use_ref[1:2, :] = w[2] * (skip * h1)
            continue
        x0, x1 = edge_ref[2 * index - 2 : 2 * index - 1], edge_ref[2 * index - 1 : 2 * index]
        f0 = w[0] * x0 + w[1] * (near * h1) + w[2] * (far * h2)
        f1 = w[0] * x1 + w[1] * (step * x0) + w[2] * (skip * h1)
        made.append((f0, f1))
    u0 = (made[0][0] * made[1][0]).astype(BF).astype(F32)
    u1 = (made[0][1] * made[1][1]).astype(BF).astype(F32)
    head_ref[0:1, :] = u0
    head_ref[1:2, :] = u1
    u0 = same(s0, end) * u0
    u1 = same(s1, end) * u1
    half = width // 2
    for part in range(2):
        at = slice(part * half, (part + 1) * half)
        rate = rate_ref[:, at]
        drop = jnp.exp(-rate * (count - 2.0))
        total_ref[part] = (sum_ref[:, at] + drop * (u1[:, at] + jnp.exp(-rate) * u0[:, at])).astype(BF)


def plan_kernel(count, rounds, pos_ref, seg_ref, ids_ref, rates_ref, res_ref, rate_ref, col_ref,
                wide_ref, lead_ref, tri_ref, keep_ref, half_ref, full_ref):
    pos = pos_ref[0]
    modes = rates_ref.shape[0]
    width = rate_ref.shape[1]
    members = width // rates_ref.shape[1]

    def seg_at(spot):
        at = jnp.maximum(spot, 0)
        return jnp.where(spot < 0, 0, ids_ref[at])

    first = pos * count
    col = col_ref[1]
    start = iota((count, LANES), 0) // SUB
    lead = jnp.zeros((count, LANES), F32)
    for c in range(count // SUB):
        lead = jnp.where(start == c, seg_at(first + c * SUB - 1).astype(F32), lead)
    lead_ref[...] = flag(col == lead).astype(BF)
    inner = lax.rem(iota((SUB, SET), 1), SUB)
    tall = iota((SUB, SET), 0)
    for c in range(count // SUB):
        row = seg_ref[pl.ds((count // LANES) * pos + c * SUB // LANES, 1), :].astype(F32)
        shift = (c * SUB) % LANES
        base = row if shift == 0 else pltpu.roll(row, LANES - shift, 1)
        base = jnp.where(iota((1, LANES), 1) < SUB, base, 0.0)
        base = base + pltpu.roll(base, SUB, 1)
        base = base + pltpu.roll(base, 2 * SUB, 1)
        base = jnp.concatenate([base] * (SET // LANES), axis=1)
        mine = jnp.concatenate([col[c * SUB : (c + 1) * SUB]] * (SET // LANES), axis=1)
        tri_ref[c * SUB : (c + 1) * SUB, :] = flag((tall >= inner) & (mine == base)).astype(BF)
        keep_ref[c * modes : (c + 1) * modes, :] = jnp.broadcast_to(
            flag(base == ids_ref[first + (c + 1) * SUB - 1].astype(F32)), (modes, SET)).astype(BF)
    weight = res_ref[...] * jnp.sqrt(rates_ref[...])
    per = LANES * members
    onehot = flag(iota((LANES, per), 0) == iota((LANES, per), 1) // members).astype(BF)
    pick = iota((modes, per), 0) == lax.rem(iota((modes, per), 1), modes)
    for block in range(width // per):
        at = slice(block * LANES, (block + 1) * LANES)
        to = slice(block * per, (block + 1) * per)
        (spread,) = spread_out([weight[:, at]], onehot)
        wide_ref[:, to] = jnp.sum(jnp.where(pick, spread, 0.0), axis=0, keepdims=True)

    def decay(rate, low, high):
        alive = flag(seg_at(low * count - 1) == seg_at(high * count - 1))
        return jnp.exp(-rate * (count * (high - low)).astype(F32)) * alive

    core = lax.rem(pos, 2)
    chip = pos // 2
    rate = rate_ref[:, pl.ds(pl.multiple_of(core * (width // 2), LANES), width // 2)]
    half_ref[0] = decay(rate, 2 * chip + 1, 2 * chip + 2)
    spot = 1
    reach = 1
    for radix in rounds:
        size = reach * radix
        top = 2 * (chip // size) * size + 2 * size
        own = 2 * (chip // reach) * reach + 2 * reach
        half_ref[spot] = decay(rate, own, top)
        for other in range(1, radix):
            group = (chip // reach) ^ other
            finish = 2 * (group + 1) * reach
            ahead = group < chip // reach
            half_ref[spot + 1] = flag(ahead) * decay(rate, jnp.where(ahead, finish, 0), 2 * chip)
            half_ref[spot + 2] = decay(rate, finish, top)
            spot += 2
        spot += 1
        reach = size
    rate = rate_ref[...]
    full_ref[0] = jnp.where(core == 0, 1.0, decay(rate, 2 * chip, 2 * chip + 1))
    full_ref[1] = decay(rate, jnp.zeros_like(pos), pos)


def local_kernel(base, u_ref, head_ref, q_ref, halo_ref, sw_ref, skip_ref, rates_ref, res_ref, rate_ref, flat_ref,
                 wide_ref, lead_ref, col_ref, tri_ref, keep_ref, out_ref, gate_ref, cross_ref):
    count, wide = out_ref.shape
    modes = rates_ref.shape[0]
    members = 16
    groups = LANES // members
    spans = count // SUB
    first = base // members
    block = slice(first // LANES * LANES, first // LANES * LANES + LANES)
    cols = wide // members * SUB
    lane = iota((1, cols), 1)
    rates = rates_ref[:, block]
    weight = res_ref[:, block] * jnp.sqrt(rates)
    filt = lane // SUB + first % LANES
    onehot = flag(iota((LANES, cols), 0) == filt).astype(BF)
    (rate_to_end,) = spread_out([rates], onehot)
    decays = jnp.exp(-rate_to_end * (SUB - 1.0 - lax.rem(lane, SUB).astype(F32))).astype(BF)
    spot = lax.rem(lane, LANES)
    within = lax.rem((spot + SUB - 1) // SUB, LANES // SUB)
    lag = jnp.where(spot == 0, 0, lax.rem(SUB - lax.rem(spot, SUB), SUB)).astype(F32)
    filt = (lane // LANES) * (LANES // SUB) + within + first % LANES
    onehot = flag(iota((LANES, cols), 0) == filt).astype(BF)
    rate_tap, weight_tap = spread_out([rates, weight], onehot)
    taps = jnp.sum(weight_tap * jnp.exp(-rate_tap * lag), axis=0, keepdims=True)

    token = iota((16, LANES), 0)
    pad = lambda x, rows: jnp.concatenate([x, jnp.zeros((rows - x.shape[0], x.shape[1]), F32)], axis=0)
    owns = flag(iota((groups * SUB, LANES), 0) // SUB == iota((groups * SUB, LANES), 1) // members).astype(BF)
    holds = flag(iota((groups * modes, LANES), 0) // modes == iota((groups * modes, LANES), 1) // members).astype(BF)
    for tile in range(wide // LANES):
        at = slice(tile * LANES, (tile + 1) * LANES)
        to = slice(base + tile * LANES, base + (tile + 1) * LANES)
        ub = u_ref[:, to]
        start = jnp.where(token < 2, pad(head_ref[:, to], 16), ub[:16].astype(F32)).astype(BF)
        ub = jnp.concatenate([start, ub[16:]], axis=0)
        rflat, wflat = flat_ref[:, to], wide_ref[:, to]
        near = []
        for part in range(SET // LANES):
            row = taps[:, tile * SET + part * LANES : tile * SET + (part + 1) * LANES]
            near.append(pltpu.roll(jnp.broadcast_to(row, (SUB, LANES)), 0, 1, stride=1, stride_axis=0))
        near = jnp.concatenate(near, axis=1).astype(BF)
        ends = decays[:, tile * SET : (tile + 1) * SET]
        table = wflat * jnp.exp(-rflat * (iota((SUB, LANES), 0).astype(F32) + 1.0))
        fall = jnp.exp(-rate_ref[:, to] * float(SUB))
        far = jnp.exp(-rflat * (SUB * iota((spans, LANES), 0).astype(F32)))
        inner, sums = [], []
        for c in range(spans):
            rows = slice(c * SUB, (c + 1) * SUB)
            left = jnp.concatenate([near * tri_ref[rows], ends * keep_ref[c * 16 : (c + 1) * 16]], axis=0)
            right = jnp.concatenate([ub[rows]] * groups, axis=0) * owns
            got = jnp.dot(left, right, preferred_element_type=F32)
            inner.append(got[:SUB])
            sums.append(got[SUB:])
            cross_ref[rows, at] = (table * far[c : c + 1] * col_ref[0, rows]).astype(BF)
        tableb = table.astype(BF)
        state = sums[0]
        local = [inner[0]]
        for c in range(1, spans):
            rows = slice(c * SUB, (c + 1) * SUB)
            reach = lead_ref[rows].astype(F32)
            right = jnp.concatenate([state.astype(BF)] * groups, axis=0) * holds
            local.append(inner[c] + jnp.dot(tableb * lead_ref[rows], right, preferred_element_type=F32))
            state = fall * reach[SUB - 1 :] * state + sums[c]
        x = q_ref[:, to].astype(F32)
        q = (
            sw_ref[0, 0:1, to] * x
            + sw_ref[1, 0:1, to] * (col_ref[2] * pltpu.roll(x, 1, 0))
            + sw_ref[2, 0:1, to] * (col_ref[3] * pltpu.roll(x, 2, 0))
        )
        q = jnp.concatenate([q[:8] + pad(halo_ref[:, to], 8), q[8:]], axis=0)
        gate_ref[:, at] = q
        out_ref[:, at] = q * (jnp.concatenate(local, axis=0) + skip_ref[:, to] * ub.astype(F32))


def last_kernel(pieces, state_ref, *refs):
    modes = state_ref.shape[0]
    members = 16
    groups = SET // members
    owner = iota((modes, SET), 1) // members
    out_ref, made_ref, sems = refs[3 * pieces :]
    copies = []
    for piece in range(pieces):
        part_ref, gate_ref, table_ref = refs[3 * piece : 3 * piece + 3]
        wide = part_ref.shape[1]
        for half in range(wide // SET):
            at = slice(half * SET, (half + 1) * SET)
            to = slice(piece * wide + half * SET, piece * wide + (half + 1) * SET)
            state = state_ref[:, to]
            spread = jnp.concatenate([jnp.where(owner == g, state, 0.0).astype(BF) for g in range(groups)], axis=0)
            cross = jnp.dot(table_ref[:, at], spread, preferred_element_type=F32)
            made_ref[:, to] = (part_ref[:, at] + gate_ref[:, at] * cross).astype(BF)
        to = slice(piece * wide, (piece + 1) * wide)
        copies.append(pltpu.make_async_copy(made_ref.at[:, to], out_ref.at[:, to], sems.at[piece]))
        copies[-1].start()
    for copy in copies:
        copy.wait()


def params(limit=16 << 20):
    return pltpu.CompilerParams(vmem_limit_bytes=limit)


def body(features, short_weight, residues, rates, skip, carry_state, earlier_rows, segment_ids):
    count, _, width = features.shape
    groups, modes = rates.shape
    blocks = lax.axis_size("ctx")
    pos = lax.axis_index("ctx")
    pos1 = pos.reshape(1)
    chips = blocks // 2
    bits = chips.bit_length() - 1
    rounds = ([4] if bits > 1 else []) + [2] * (bits - 2 if bits > 1 else bits)
    assert blocks == 2 << bits and count == 2 * LANES and width == 16 * groups and modes == 16
    feat = jnp.transpose(features, (1, 0, 2))
    early = jnp.transpose(earlier_rows, (1, 0, 2))
    segs = segment_ids.reshape(-1, LANES)
    rates_t = rates.T
    res_t = residues.T
    skip = skip.reshape(1, width)
    vm = pl.BlockSpec(memory_space=pltpu.VMEM)
    sm = pl.BlockSpec(memory_space=pltpu.SMEM)
    out = lambda *shape, dtype=F32: jax.ShapeDtypeStruct(shape, dtype)
    stay = lambda value: pltpu.with_memory_space_constraint(value, pltpu.HBM)
    swap = lambda value, by: lax.ppermute(value, "ctx", [(i, i ^ by) for i in range(blocks)])
    tie = lambda *values: lax.optimization_barrier(values)

    halo = lax.ppermute(feat[:, count - 2 :], "ctx", [(i, i + 1) for i in range(blocks - 1)])

    hbm = pl.BlockSpec(memory_space=pltpu.HBM)
    u, q, sums, rate, flat, edge, cols, weights = pl.pallas_call(
        first_kernel,
        in_specs=[sm, hbm, hbm, hbm, hbm],
        out_specs=[vm] * 8,
        out_shape=[out(count, width, dtype=BF), out(count, width, dtype=BF), out(modes, width), out(modes, width),
                   out(1, width), out(4, width), out(4, count, LANES),
                   out(*short_weight.shape)],
        scratch_shapes=[
            pltpu.VMEM((count, LANES), BF), pltpu.VMEM((2 * count, count), BF), pltpu.VMEM((2, count, width), BF), pltpu.VMEM(segs.shape, jnp.int32),
            pltpu.VMEM(rates_t.shape, F32), pltpu.SemaphoreType.DMA((2 * (width // WIDE) + 4,)),
        ],
        compiler_params=params(),
        name="first",
    )(pos1, stay(segs), stay(rates_t), stay(feat), stay(short_weight))

    total, head, halo_q = pl.pallas_call(
        lambda *refs: head_kernel(count, *refs),
        in_specs=[sm] + [vm] * 7,
        out_specs=[vm] * 3,
        out_shape=[out(2, modes, width // 2, dtype=BF), out(2, width), out(2, width)],
        compiler_params=params(),
        name="head",
    )(pos1, segs, edge, halo, early, weights, rate, sums)

    even = (pos & 1) == 0
    other = swap(total, 1)
    steps = 1 + sum(2 * radix - 1 for radix in rounds)
    wflat, lead, tris, keeps, halves, fulls = pl.pallas_call(
        lambda *refs: plan_kernel(count, rounds, *refs),
        in_specs=[sm, vm, sm] + [vm] * 4,
        out_specs=[vm] * 6,
        out_shape=[
            out(1, width), out(count, LANES, dtype=BF), out(count, SET, dtype=BF), out(count // SUB * 16, SET, dtype=BF),
            out(steps, modes, width // 2), out(2, modes, width),
        ],
        compiler_params=params(),
        cost_estimate=pl.CostEstimate(flops=1 << 30, bytes_accessed=5 << 20, transcendentals=0),
        name="plan",
    )(pos1, segs, segment_ids, rates_t, res_t, rate, cols)

    pieces = width // WIDE
    parts = []

    def local(piece, head):
        return pl.pallas_call(
            lambda *refs: local_kernel(piece * WIDE, *refs),
            in_specs=[vm] * 15,
            out_specs=[vm] * 3,
            out_shape=[out(count, WIDE), out(count, WIDE), out(count, WIDE, dtype=BF)],
            compiler_params=params(),
            cost_estimate=pl.CostEstimate(flops=4 << 30, bytes_accessed=5 << 20, transcendentals=0),
            name="local",
        )(u, head, q, halo_q, weights, skip, rates_t, res_t, rate, flat, wflat, lead, cols, tris, keeps)

    low_total = jnp.where(even, total, other)
    own_half = lambda value: jnp.where(even, value[0], value[1]).astype(F32)
    chip_total = halves[0] * own_half(low_total) + own_half(jnp.where(even, other, total))
    chip_total, head = tie(chip_total, head)
    before = jnp.zeros_like(chip_total)
    spot, reach = 1, 1
    left = list(range(pieces))
    for number, radix in enumerate(rounds):
        sent = chip_total.astype(BF)
        got = [swap(sent, 2 * reach * i).astype(F32) for i in range(1, radix)]
        share = -(-len(left) // (len(rounds) - number))
        for piece in left[:share]:
            parts.append(local(piece, head))
        left = left[share:]
        got, parts, head = tie(got, parts, head)
        chip_total = halves[spot] * chip_total
        for i in range(radix - 1):
            before = before + halves[spot + 1 + 2 * i] * got[i]
            chip_total = chip_total + halves[spot + 2 + 2 * i] * got[i]
        spot += 2 * radix - 1
        reach *= radix
    mine = before.astype(BF)
    yours = swap(mine, 1)
    full = jnp.concatenate([jnp.where(even, mine, yours), jnp.where(even, yours, mine)], axis=1).astype(F32)
    low_full = jnp.where(even, 0.0, jnp.concatenate([low_total[0], low_total[1]], axis=1).astype(F32))
    state = fulls[0] * full + low_full + fulls[1] * carry_state

    return pl.pallas_call(
        lambda *refs: last_kernel(pieces, *refs),
        in_specs=[vm] * (1 + 3 * pieces),
        out_specs=hbm,
        out_shape=out(count, width, dtype=BF),
        scratch_shapes=[pltpu.VMEM((count, width), BF), pltpu.SemaphoreType.DMA((pieces,))],
        compiler_params=params(),
        name="last",
    )(state, *[value for piece in parts for value in piece])


def solution(mesh):
    placed = (
        P(("groups", "ctx"), None, None),
        P(),
        P(),
        P(),
        P(),
        P("groups", None),
        P("groups", None, None),
        P("groups"),
    )
    return jax.shard_map(
        body, mesh=mesh, in_specs=placed, out_specs=P(("groups", "ctx"), None), check_vma=False
    )
```

```python
import jax
import jax.numpy as jnp
from jax import lax
from jax.experimental import pallas as pl
from jax.experimental.pallas import tpu as pltpu
from jax.sharding import PartitionSpec as P

BF = jnp.bfloat16
F32 = jnp.float32
LANES = 128
SET = 256
WIDE = 1024
SUB = 32


def iota(shape, dim):
    return lax.broadcasted_iota(jnp.int32, shape, dim)


def flag(x):
    return x.astype(F32)


def split3(x):
    hi = x.astype(BF)
    rest = x - hi.astype(F32)
    mid = rest.astype(BF)
    low = (rest - mid.astype(F32)).astype(BF)
    return [hi, mid, low]


def spread_out(values, onehot):
    rows = values[0].shape[0]
    pieces = sum([split3(value) for value in values], [])
    got = jnp.dot(jnp.concatenate(pieces, axis=0), onehot, preferred_element_type=F32)
    part = lambda i: got[i * rows : (i + 1) * rows]
    return [(part(3 * i) + part(3 * i + 1)) + part(3 * i + 2) for i in range(len(values))]


def first_kernel(pos_ref, seg_hbm, rates_hbm, feat_ref, taps_hbm,
                 u_ref, q_ref, sum_ref, rate_ref, flat_ref, edge_ref, col_ref, taps_ref,
                 keep_ref, shift_ref, kv_ref, seg_ref, rates_ref, sems):
    pos = pos_ref[0]
    count, width = u_ref.shape
    modes = sum_ref.shape[0]
    members = SET // modes
    chunks = width // WIDE

    def copies(chunk):
        at = slice(chunk * WIDE, (chunk + 1) * WIDE)
        return [
            pltpu.make_async_copy(feat_ref.at[1 + i, :, at], kv_ref.at[i, :, at], sems.at[2 * chunk + i])
            for i in range(2)
        ]

    small = [
        pltpu.make_async_copy(source, target, sems.at[2 * chunks + i])
        for i, (source, target) in enumerate(((seg_hbm, seg_ref), (rates_hbm, rates_ref), (taps_hbm, taps_ref)))
    ]
    q_copy = pltpu.make_async_copy(feat_ref.at[0], q_ref, sems.at[2 * chunks + 3])
    for copy in small:
        copy.start()
    for chunk in range(chunks):
        for copy in copies(chunk):
            copy.start()
    q_copy.start()
    for copy in small:
        copy.wait()

    @pl.when(pos >= 0)
    def _():
        token = iota((count, LANES), 0)
        halves, rows = [], []
        for part in range(count // LANES):
            row = seg_ref[pl.ds((count // LANES) * pos + part, 1), :].astype(F32)
            rows.append(row)
            halves.append(jnp.transpose(jnp.broadcast_to(row, (LANES, LANES))))
        col = jnp.concatenate(halves, axis=0)
        before = seg_ref[pl.ds(jnp.maximum((count // LANES) * pos - 1, 0), 1), :].astype(F32)
        before = jnp.where(pos == 0, 0.0, before)
        last = jnp.broadcast_to(before[:, LANES - 1 :], (1, LANES))
        end = jnp.broadcast_to(rows[-1][:, LANES - 1 :], (1, LANES))
        col_ref[0] = flag(col == last)
        col_ref[1] = col
        keep_ref[...] = flag((col == end) & (token >= 2)).astype(BF)
        col_ref[2] = flag((col == pltpu.roll(col, 1, 0)) & (token >= 1))
        col_ref[3] = flag((col == pltpu.roll(col, 2, 0)) & (token >= 2))
        every = jnp.concatenate(rows, axis=1)
        there = jnp.concatenate([col] * (count // LANES), axis=1)
        gap = iota((count, count), 0) - iota((count, count), 1)
        for step in (1, 2):
            shift_ref[(step - 1) * count : step * count, :] = flag((gap == step) & (there == every)).astype(BF)

        per = LANES * members
        onehot = flag(iota((LANES, per), 0) == iota((LANES, per), 1) // members).astype(BF)
        pick = iota((modes, per), 0) == lax.rem(iota((modes, per), 1), modes)
        for block in range(width // per):
            at = slice(block * LANES, (block + 1) * LANES)
            to = slice(block * per, (block + 1) * per)
            (rate,) = spread_out([rates_ref[:, at]], onehot)
            rate_ref[:, to] = rate
            flat_ref[:, to] = jnp.sum(jnp.where(pick, rate, 0.0), axis=0, keepdims=True)

    owner = iota((modes, LANES), 1) // members
    spans = count // SUB

    def two_tiles(start):
        both = pl.ds(start, SET)
        shifted = []
        for index in (1, 2):
            edge_ref[2 * index - 2 : 2 * index, both] = kv_ref[index - 1, :16, both].astype(F32)[:2]
            shifted.append(jnp.dot(shift_ref[...], kv_ref[index - 1, :, both], preferred_element_type=F32))
        for part in range(SET // LANES):
            at = pl.ds(start + part * LANES, LANES)
            cut = slice(part * LANES, (part + 1) * LANES)
            made = []
            for index in (1, 2):
                moved = shifted[index - 1]
                made.append(
                    taps_ref[0, index : index + 1, at] * kv_ref[index - 1, :, at].astype(F32)
                    + taps_ref[1, index : index + 1, at] * moved[:count, cut]
                    + taps_ref[2, index : index + 1, at] * moved[count:, cut]
                )
            u = (made[0] * made[1]).astype(BF)
            u_ref[:, at] = u

    def sums_of(start):
        at = pl.ds(start, SET)
        rflat = flat_ref[:, at]
        fine = jnp.exp(-rflat * (SUB - 1.0 - iota((SUB, SET), 0).astype(F32)))
        coarse = jnp.exp(-rflat * (SUB * (spans - 1.0 - iota((spans, SET), 0).astype(F32))))
        decay = jnp.concatenate([(coarse[a : a + 1] * fine).astype(BF) for a in range(spans)], axis=0)
        decay = decay * jnp.concatenate([keep_ref[...]] * (SET // LANES), axis=1)
        sums = lax.dot_general(decay, u_ref[:, at], (((0,), (0,)), ((), ())), preferred_element_type=F32)
        for part in range(SET // LANES):
            cut = slice(part * LANES, (part + 1) * LANES)
            total = jnp.zeros((modes, LANES), F32)
            for g in range(LANES // members):
                row = part * LANES + g * modes
                total = jnp.where(owner == g, sums[row : row + modes, cut], total)
            sum_ref[:, pl.ds(start + part * LANES, LANES)] = total

    for chunk in range(chunks):
        for copy in copies(chunk):
            copy.wait()

        @pl.when(pos >= 0)
        def _():
            for i in range(WIDE // SET):
                two_tiles(chunk * WIDE + i * SET)

    @pl.when(pos >= 0)
    def _():
        for i in range(width // SET):
            sums_of(i * SET)

    q_copy.wait()


def head_kernel(count, pos_ref, seg_ref, edge_ref, halo_ref, early_ref, sw_ref, rate_ref, sum_ref, q_ref,
                total_ref, head_ref, use_ref, same_ref):
    pos = pos_ref[0]
    width = rate_ref.shape[1]
    per = count // LANES
    row = seg_ref[pl.ds(per * pos, 1), :]
    tail = seg_ref[pl.ds(per * pos + per - 1, 1), :]
    before = seg_ref[pl.ds(jnp.maximum(per * pos - 1, 0), 1), :]
    before = jnp.where(pos == 0, 0, before)
    s0, s1 = row[:, 0:1], row[:, 1:2]
    end = tail[:, LANES - 1 :]
    p1, p2 = before[:, LANES - 1 :], before[:, LANES - 2 : LANES - 1]
    same = lambda a, b: jnp.broadcast_to(flag(a == b), (1, width))
    near, far = same(p1, s0), same(p2, s0)
    step, skip = same(s0, s1), same(p1, s1)
    made = []
    for index in (0, 1, 2):
        h = jnp.where(pos == 0, early_ref[index].astype(F32), halo_ref[index].astype(F32))
        h2, h1 = h[0:1], h[1:2]
        w = [sw_ref[j, index : index + 1, :] for j in range(3)]
        if index == 0:
            use_ref[0:1, :] = w[1] * (near * h1) + w[2] * (far * h2)
            use_ref[1:2, :] = w[2] * (skip * h1)
            continue
        x0, x1 = edge_ref[2 * index - 2 : 2 * index - 1], edge_ref[2 * index - 1 : 2 * index]
        f0 = w[0] * x0 + w[1] * (near * h1) + w[2] * (far * h2)
        f1 = w[0] * x1 + w[1] * (step * x0) + w[2] * (skip * h1)
        made.append((f0, f1))
    u0 = (made[0][0] * made[1][0]).astype(BF).astype(F32)
    u1 = (made[0][1] * made[1][1]).astype(BF).astype(F32)
    head_ref[0:1, :] = u0
    head_ref[1:2, :] = u1
    u0 = same(s0, end) * u0
    u1 = same(s1, end) * u1
    half = width // 2
    for part in range(2):
        at = slice(part * half, (part + 1) * half)
        rate = rate_ref[:, at]
        drop = jnp.exp(-rate * (count - 2.0))
        total_ref[part] = (sum_ref[:, at] + drop * (u1[:, at] + jnp.exp(-rate) * u0[:, at])).astype(BF)


def plan_kernel(count, rounds, pos_ref, seg_ref, ids_ref, rates_ref, res_ref, rate_ref, col_ref,
                wide_ref, lead_ref, tri_ref, keep_ref, half_ref, full_ref):
    pos = pos_ref[0]
    modes = rates_ref.shape[0]
    width = rate_ref.shape[1]
    members = width // rates_ref.shape[1]

    def seg_at(spot):
        at = jnp.maximum(spot, 0)
        return jnp.where(spot < 0, 0, ids_ref[at])

    first = pos * count
    col = col_ref[1]
    start = iota((count, LANES), 0) // SUB
    lead = jnp.zeros((count, LANES), F32)
    for c in range(count // SUB):
        lead = jnp.where(start == c, seg_at(first + c * SUB - 1).astype(F32), lead)
    lead_ref[...] = flag(col == lead).astype(BF)
    inner = lax.rem(iota((SUB, SET), 1), SUB)
    tall = iota((SUB, SET), 0)
    for c in range(count // SUB):
        row = seg_ref[pl.ds((count // LANES) * pos + c * SUB // LANES, 1), :].astype(F32)
        shift = (c * SUB) % LANES
        base = row if shift == 0 else pltpu.roll(row, LANES - shift, 1)
        base = jnp.where(iota((1, LANES), 1) < SUB, base, 0.0)
        base = base + pltpu.roll(base, SUB, 1)
        base = base + pltpu.roll(base, 2 * SUB, 1)
        base = jnp.concatenate([base] * (SET // LANES), axis=1)
        mine = jnp.concatenate([col[c * SUB : (c + 1) * SUB]] * (SET // LANES), axis=1)
        tri_ref[c * SUB : (c + 1) * SUB, :] = flag((tall >= inner) & (mine == base)).astype(BF)
        keep_ref[c * modes : (c + 1) * modes, :] = jnp.broadcast_to(
            flag(base == ids_ref[first + (c + 1) * SUB - 1].astype(F32)), (modes, SET)).astype(BF)
    weight = res_ref[...] * jnp.sqrt(rates_ref[...])
    per = LANES * members
    onehot = flag(iota((LANES, per), 0) == iota((LANES, per), 1) // members).astype(BF)
    pick = iota((modes, per), 0) == lax.rem(iota((modes, per), 1), modes)
    for block in range(width // per):
        at = slice(block * LANES, (block + 1) * LANES)
        to = slice(block * per, (block + 1) * per)
        (spread,) = spread_out([weight[:, at]], onehot)
        wide_ref[:, to] = jnp.sum(jnp.where(pick, spread, 0.0), axis=0, keepdims=True)

    def decay(rate, low, high):
        alive = flag(seg_at(low * count - 1) == seg_at(high * count - 1))
        return jnp.exp(-rate * (count * (high - low)).astype(F32)) * alive

    core = lax.rem(pos, 2)
    chip = pos // 2
    rate = rate_ref[:, pl.ds(pl.multiple_of(core * (width // 2), LANES), width // 2)]
    half_ref[0] = decay(rate, 2 * chip + 1, 2 * chip + 2)
    spot = 1
    reach = 1
    for radix in rounds:
        size = reach * radix
        top = 2 * (chip // size) * size + 2 * size
        own = 2 * (chip // reach) * reach + 2 * reach
        half_ref[spot] = decay(rate, own, top)
        for other in range(1, radix):
            group = (chip // reach) ^ other
            finish = 2 * (group + 1) * reach
            ahead = group < chip // reach
            half_ref[spot + 1] = flag(ahead) * decay(rate, jnp.where(ahead, finish, 0), 2 * chip)
            half_ref[spot + 2] = decay(rate, finish, top)
            spot += 2
        spot += 1
        reach = size
    rate = rate_ref[...]
    full_ref[0] = jnp.where(core == 0, 1.0, decay(rate, 2 * chip, 2 * chip + 1))
    full_ref[1] = decay(rate, jnp.zeros_like(pos), pos)


def local_kernel(base, u_ref, head_ref, q_ref, halo_ref, sw_ref, skip_ref, rates_ref, res_ref, rate_ref, flat_ref,
                 wide_ref, lead_ref, col_ref, tri_ref, keep_ref, out_ref, gate_ref, cross_ref):
    count, wide = out_ref.shape
    modes = rates_ref.shape[0]
    members = 16
    groups = LANES // members
    spans = count // SUB
    first = base // members
    block = slice(first // LANES * LANES, first // LANES * LANES + LANES)
    cols = wide // members * SUB
    lane = iota((1, cols), 1)
    rates = rates_ref[:, block]
    weight = res_ref[:, block] * jnp.sqrt(rates)
    filt = lane // SUB + first % LANES
    onehot = flag(iota((LANES, cols), 0) == filt).astype(BF)
    (rate_to_end,) = spread_out([rates], onehot)
    decays = jnp.exp(-rate_to_end * (SUB - 1.0 - lax.rem(lane, SUB).astype(F32))).astype(BF)
    spot = lax.rem(lane, LANES)
    within = lax.rem((spot + SUB - 1) // SUB, LANES // SUB)
    lag = jnp.where(spot == 0, 0, lax.rem(SUB - lax.rem(spot, SUB), SUB)).astype(F32)
    filt = (lane // LANES) * (LANES // SUB) + within + first % LANES
    onehot = flag(iota((LANES, cols), 0) == filt).astype(BF)
    rate_tap, weight_tap = spread_out([rates, weight], onehot)
    taps = jnp.sum(weight_tap * jnp.exp(-rate_tap * lag), axis=0, keepdims=True)

    token = iota((16, LANES), 0)
    pad = lambda x, rows: jnp.concatenate([x, jnp.zeros((rows - x.shape[0], x.shape[1]), F32)], axis=0)
    owns = flag(iota((groups * SUB, LANES), 0) // SUB == iota((groups * SUB, LANES), 1) // members).astype(BF)
    holds = flag(iota((groups * modes, LANES), 0) // modes == iota((groups * modes, LANES), 1) // members).astype(BF)
    for tile in range(wide // LANES):
        at = slice(tile * LANES, (tile + 1) * LANES)
        to = slice(base + tile * LANES, base + (tile + 1) * LANES)
        ub = u_ref[:, to]
        start = jnp.where(token < 2, pad(head_ref[:, to], 16), ub[:16].astype(F32)).astype(BF)
        ub = jnp.concatenate([start, ub[16:]], axis=0)
        rflat, wflat = flat_ref[:, to], wide_ref[:, to]
        near = []
        for part in range(SET // LANES):
            row = taps[:, tile * SET + part * LANES : tile * SET + (part + 1) * LANES]
            near.append(pltpu.roll(jnp.broadcast_to(row, (SUB, LANES)), 0, 1, stride=1, stride_axis=0))
        near = jnp.concatenate(near, axis=1).astype(BF)
        ends = decays[:, tile * SET : (tile + 1) * SET]
        table = wflat * jnp.exp(-rflat * (iota((SUB, LANES), 0).astype(F32) + 1.0))
        fall = jnp.exp(-rate_ref[:, to] * float(SUB))
        far = jnp.exp(-rflat * (SUB * iota((spans, LANES), 0).astype(F32)))
        inner, sums = [], []
        for c in range(spans):
            rows = slice(c * SUB, (c + 1) * SUB)
            left = jnp.concatenate([near * tri_ref[rows], ends * keep_ref[c * 16 : (c + 1) * 16]], axis=0)
            right = jnp.concatenate([ub[rows]] * groups, axis=0) * owns
            got = jnp.dot(left, right, preferred_element_type=F32)
            inner.append(got[:SUB])
            sums.append(got[SUB:])
            cross_ref[rows, at] = (table * far[c : c + 1] * col_ref[0, rows]).astype(BF)
        tableb = table.astype(BF)
        state = sums[0]
        local = [inner[0]]
        for c in range(1, spans):
            rows = slice(c * SUB, (c + 1) * SUB)
            reach = lead_ref[rows].astype(F32)
            right = jnp.concatenate([state.astype(BF)] * groups, axis=0) * holds
            local.append(inner[c] + jnp.dot(tableb * lead_ref[rows], right, preferred_element_type=F32))
            state = fall * reach[SUB - 1 :] * state + sums[c]
        x = q_ref[:, to].astype(F32)
        q = (
            sw_ref[0, 0:1, to] * x
            + sw_ref[1, 0:1, to] * (col_ref[2] * pltpu.roll(x, 1, 0))
            + sw_ref[2, 0:1, to] * (col_ref[3] * pltpu.roll(x, 2, 0))
        )
        q = jnp.concatenate([q[:8] + pad(halo_ref[:, to], 8), q[8:]], axis=0)
        gate_ref[:, at] = q
        out_ref[:, at] = q * (jnp.concatenate(local, axis=0) + skip_ref[:, to] * ub.astype(F32))


def last_kernel(pieces, state_ref, *refs):
    modes = state_ref.shape[0]
    members = 16
    groups = SET // members
    owner = iota((modes, SET), 1) // members
    out_ref, made_ref, sems = refs[3 * pieces :]
    copies = []
    for piece in range(pieces):
        part_ref, gate_ref, table_ref = refs[3 * piece : 3 * piece + 3]
        wide = part_ref.shape[1]
        for half in range(wide // SET):
            at = slice(half * SET, (half + 1) * SET)
            to = slice(piece * wide + half * SET, piece * wide + (half + 1) * SET)
            state = state_ref[:, to]
            spread = jnp.concatenate([jnp.where(owner == g, state, 0.0).astype(BF) for g in range(groups)], axis=0)
            cross = jnp.dot(table_ref[:, at], spread, preferred_element_type=F32)
            made_ref[:, to] = (part_ref[:, at] + gate_ref[:, at] * cross).astype(BF)
        to = slice(piece * wide, (piece + 1) * wide)
        copies.append(pltpu.make_async_copy(made_ref.at[:, to], out_ref.at[:, to], sems.at[piece]))
        copies[-1].start()
    for copy in copies:
        copy.wait()


def params(limit=16 << 20):
    return pltpu.CompilerParams(vmem_limit_bytes=limit)


def body(features, short_weight, residues, rates, skip, carry_state, earlier_rows, segment_ids):
    count, _, width = features.shape
    groups, modes = rates.shape
    blocks = lax.axis_size("ctx")
    pos = lax.axis_index("ctx")
    pos1 = pos.reshape(1)
    chips = blocks // 2
    bits = chips.bit_length() - 1
    rounds = ([4] if bits > 1 else []) + [2] * (bits - 2 if bits > 1 else bits)
    assert blocks == 2 << bits and count == 2 * LANES and width == 16 * groups and modes == 16
    feat = jnp.transpose(features, (1, 0, 2))
    early = jnp.transpose(earlier_rows, (1, 0, 2))
    segs = segment_ids.reshape(-1, LANES)
    rates_t = rates.T
    res_t = residues.T
    skip = skip.reshape(1, width)
    vm = pl.BlockSpec(memory_space=pltpu.VMEM)
    sm = pl.BlockSpec(memory_space=pltpu.SMEM)
    out = lambda *shape, dtype=F32: jax.ShapeDtypeStruct(shape, dtype)
    stay = lambda value: pltpu.with_memory_space_constraint(value, pltpu.HBM)
    swap = lambda value, by: lax.ppermute(value, "ctx", [(i, i ^ by) for i in range(blocks)])
    tie = lambda *values: lax.optimization_barrier(values)

    halo = lax.ppermute(feat[:, count - 2 :], "ctx", [(i, i + 1) for i in range(blocks - 1)])

    hbm = pl.BlockSpec(memory_space=pltpu.HBM)
    u, q, sums, rate, flat, edge, cols, weights = pl.pallas_call(
        first_kernel,
        in_specs=[sm, hbm, hbm, hbm, hbm],
        out_specs=[vm] * 8,
        out_shape=[out(count, width, dtype=BF), out(count, width, dtype=BF), out(modes, width), out(modes, width),
                   out(1, width), out(4, width), out(4, count, LANES),
                   out(*short_weight.shape)],
        scratch_shapes=[
            pltpu.VMEM((count, LANES), BF), pltpu.VMEM((2 * count, count), BF), pltpu.VMEM((2, count, width), BF), pltpu.VMEM(segs.shape, jnp.int32),
            pltpu.VMEM(rates_t.shape, F32), pltpu.SemaphoreType.DMA((2 * (width // WIDE) + 4,)),
        ],
        compiler_params=params(),
        name="first",
    )(pos1, stay(segs), stay(rates_t), stay(feat), stay(short_weight))

    total, head, halo_q, q = pl.pallas_call(
        lambda *refs: head_kernel(count, *refs),
        in_specs=[sm] + [vm] * 8,
        out_specs=[vm] * 4,
        out_shape=[out(2, modes, width // 2, dtype=BF), out(2, width), out(2, width), out(count, width, dtype=BF)],
        input_output_aliases={8: 3},
        compiler_params=params(),
        name="head",
    )(pos1, segs, edge, halo, early, weights, rate, sums, q)

    even = (pos & 1) == 0
    other = swap(total, 1)
    steps = 1 + sum(2 * radix - 1 for radix in rounds)
    wflat, lead, tris, keeps, halves, fulls = pl.pallas_call(
        lambda *refs: plan_kernel(count, rounds, *refs),
        in_specs=[sm, vm, sm] + [vm] * 4,
        out_specs=[vm] * 6,
        out_shape=[
            out(1, width), out(count, LANES, dtype=BF), out(count, SET, dtype=BF), out(count // SUB * 16, SET, dtype=BF),
            out(steps, modes, width // 2), out(2, modes, width),
        ],
        compiler_params=params(),
        cost_estimate=pl.CostEstimate(flops=1 << 30, bytes_accessed=5 << 20, transcendentals=0),
        name="plan",
    )(pos1, segs, segment_ids, rates_t, res_t, rate, cols)

    pieces = width // WIDE
    parts = []

    def local(piece, head):
        return pl.pallas_call(
            lambda *refs: local_kernel(piece * WIDE, *refs),
            in_specs=[vm] * 15,
            out_specs=[vm] * 3,
            out_shape=[out(count, WIDE), out(count, WIDE), out(count, WIDE, dtype=BF)],
            compiler_params=params(),
            cost_estimate=pl.CostEstimate(flops=4 << 30, bytes_accessed=5 << 20, transcendentals=0),
            name="local",
        )(u, head, q, halo_q, weights, skip, rates_t, res_t, rate, flat, wflat, lead, cols, tris, keeps)

    low_total = jnp.where(even, total, other)
    own_half = lambda value: jnp.where(even, value[0], value[1]).astype(F32)
    chip_total = halves[0] * own_half(low_total) + own_half(jnp.where(even, other, total))
    chip_total, head = tie(chip_total, head)
    before = jnp.zeros_like(chip_total)
    spot, reach = 1, 1
    left = list(range(pieces))
    for number, radix in enumerate(rounds):
        sent = chip_total.astype(BF)
        got = [swap(sent, 2 * reach * i).astype(F32) for i in range(1, radix)]
        share = -(-len(left) // (len(rounds) - number))
        for piece in left[:share]:
            parts.append(local(piece, head))
        left = left[share:]
        got, parts, head = tie(got, parts, head)
        chip_total = halves[spot] * chip_total
        for i in range(radix - 1):
            before = before + halves[spot + 1 + 2 * i] * got[i]
            chip_total = chip_total + halves[spot + 2 + 2 * i] * got[i]
        spot += 2 * radix - 1
        reach *= radix
    mine = before.astype(BF)
    yours = swap(mine, 1)
    full = jnp.concatenate([jnp.where(even, mine, yours), jnp.where(even, yours, mine)], axis=1).astype(F32)
    low_full = jnp.where(even, 0.0, jnp.concatenate([low_total[0], low_total[1]], axis=1).astype(F32))
    state = fulls[0] * full + low_full + fulls[1] * carry_state

    return pl.pallas_call(
        lambda *refs: last_kernel(pieces, *refs),
        in_specs=[vm] * (1 + 3 * pieces),
        out_specs=hbm,
        out_shape=out(count, width, dtype=BF),
        scratch_shapes=[pltpu.VMEM((count, width), BF), pltpu.SemaphoreType.DMA((pieces,))],
        compiler_params=params(),
        name="last",
    )(state, *[value for piece in parts for value in piece])


def solution(mesh):
    placed = (
        P(("groups", "ctx"), None, None),
        P(),
        P(),
        P(),
        P(),
        P("groups", None),
        P("groups", None, None),
        P("groups"),
    )
    return jax.shard_map(
        body, mesh=mesh, in_specs=placed, out_specs=P(("groups", "ctx"), None), check_vma=False
    )
```

```python
import jax
import jax.numpy as jnp
from jax import lax
from jax.experimental import pallas as pl
from jax.experimental.pallas import tpu as pltpu
from jax.sharding import PartitionSpec as P

BF = jnp.bfloat16
F32 = jnp.float32
LANES = 128
SET = 256
WIDE = 1024
PIECE = 2048
SUB = 32


def iota(shape, dim):
    return lax.broadcasted_iota(jnp.int32, shape, dim)


def flag(x):
    return x.astype(F32)


def split3(x):
    hi = x.astype(BF)
    rest = x - hi.astype(F32)
    mid = rest.astype(BF)
    low = (rest - mid.astype(F32)).astype(BF)
    return [hi, mid, low]


def spread_out(values, onehot):
    rows = values[0].shape[0]
    pieces = sum([split3(value) for value in values], [])
    got = jnp.dot(jnp.concatenate(pieces, axis=0), onehot, preferred_element_type=F32)
    part = lambda i: got[i * rows : (i + 1) * rows]
    return [(part(3 * i) + part(3 * i + 1)) + part(3 * i + 2) for i in range(len(values))]


def first_kernel(pos_ref, seg_hbm, rates_hbm, feat_ref, taps_hbm,
                 u_ref, q_ref, sum_ref, rate_ref, flat_ref, edge_ref, col_ref, taps_ref,
                 keep_ref, shift_ref, kv_ref, seg_ref, rates_ref, sems):
    pos = pos_ref[0]
    count, width = u_ref.shape
    modes = sum_ref.shape[0]
    members = SET // modes
    chunks = width // WIDE

    def copies(chunk):
        at = slice(chunk * WIDE, (chunk + 1) * WIDE)
        return [
            pltpu.make_async_copy(feat_ref.at[1 + i, :, at], kv_ref.at[i, :, at], sems.at[2 * chunk + i])
            for i in range(2)
        ]

    small = [
        pltpu.make_async_copy(source, target, sems.at[2 * chunks + i])
        for i, (source, target) in enumerate(((seg_hbm, seg_ref), (rates_hbm, rates_ref), (taps_hbm, taps_ref)))
    ]
    q_copy = pltpu.make_async_copy(feat_ref.at[0], q_ref, sems.at[2 * chunks + 3])
    for copy in small:
        copy.start()
    for chunk in range(chunks):
        for copy in copies(chunk):
            copy.start()
    q_copy.start()
    for copy in small:
        copy.wait()

    @pl.when(pos >= 0)
    def _():
        token = iota((count, LANES), 0)
        halves, rows = [], []
        for part in range(count // LANES):
            row = seg_ref[pl.ds((count // LANES) * pos + part, 1), :].astype(F32)
            rows.append(row)
            halves.append(jnp.transpose(jnp.broadcast_to(row, (LANES, LANES))))
        col = jnp.concatenate(halves, axis=0)
        before = seg_ref[pl.ds(jnp.maximum((count // LANES) * pos - 1, 0), 1), :].astype(F32)
        before = jnp.where(pos == 0, 0.0, before)
        last = jnp.broadcast_to(before[:, LANES - 1 :], (1, LANES))
        end = jnp.broadcast_to(rows[-1][:, LANES - 1 :], (1, LANES))
        col_ref[0] = flag(col == last)
        col_ref[1] = col
        keep_ref[...] = flag((col == end) & (token >= 2)).astype(BF)
        col_ref[2] = flag((col == pltpu.roll(col, 1, 0)) & (token >= 1))
        col_ref[3] = flag((col == pltpu.roll(col, 2, 0)) & (token >= 2))
        every = jnp.concatenate(rows, axis=1)
        there = jnp.concatenate([col] * (count // LANES), axis=1)
        gap = iota((count, count), 0) - iota((count, count), 1)
        for step in (1, 2):
            shift_ref[(step - 1) * count : step * count, :] = flag((gap == step) & (there == every)).astype(BF)

        per = LANES * members
        onehot = flag(iota((LANES, per), 0) == iota((LANES, per), 1) // members).astype(BF)
        pick = iota((modes, per), 0) == lax.rem(iota((modes, per), 1), modes)
        for block in range(width // per):
            at = slice(block * LANES, (block + 1) * LANES)
            to = slice(block * per, (block + 1) * per)
            (rate,) = spread_out([rates_ref[:, at]], onehot)
            rate_ref[:, to] = rate
            flat_ref[:, to] = jnp.sum(jnp.where(pick, rate, 0.0), axis=0, keepdims=True)

    owner = iota((modes, LANES), 1) // members
    spans = count // SUB

    def two_tiles(start):
        both = pl.ds(start, SET)
        shifted = []
        for index in (1, 2):
            edge_ref[2 * index - 2 : 2 * index, both] = kv_ref[index - 1, :16, both].astype(F32)[:2]
            shifted.append(jnp.dot(shift_ref[...], kv_ref[index - 1, :, both], preferred_element_type=F32))
        for part in range(SET // LANES):
            at = pl.ds(start + part * LANES, LANES)
            cut = slice(part * LANES, (part + 1) * LANES)
            made = []
            for index in (1, 2):
                moved = shifted[index - 1]
                made.append(
                    taps_ref[0, index : index + 1, at] * kv_ref[index - 1, :, at].astype(F32)
                    + taps_ref[1, index : index + 1, at] * moved[:count, cut]
                    + taps_ref[2, index : index + 1, at] * moved[count:, cut]
                )
            u = (made[0] * made[1]).astype(BF)
            u_ref[:, at] = u

    def sums_of(start):
        at = pl.ds(start, SET)
        rflat = flat_ref[:, at]
        fine = jnp.exp(-rflat * (SUB - 1.0 - iota((SUB, SET), 0).astype(F32)))
        coarse = jnp.exp(-rflat * (SUB * (spans - 1.0 - iota((spans, SET), 0).astype(F32))))
        decay = jnp.concatenate([(coarse[a : a + 1] * fine).astype(BF) for a in range(spans)], axis=0)
        decay = decay * jnp.concatenate([keep_ref[...]] * (SET // LANES), axis=1)
        sums = lax.dot_general(decay, u_ref[:, at], (((0,), (0,)), ((), ())), preferred_element_type=F32)
        for part in range(SET // LANES):
            cut = slice(part * LANES, (part + 1) * LANES)
            total = jnp.zeros((modes, LANES), F32)
            for g in range(LANES // members):
                row = part * LANES + g * modes
                total = jnp.where(owner == g, sums[row : row + modes, cut], total)
            sum_ref[:, pl.ds(start + part * LANES, LANES)] = total

    for chunk in range(chunks):
        for copy in copies(chunk):
            copy.wait()

        @pl.when(pos >= 0)
        def _():
            for i in range(WIDE // SET):
                two_tiles(chunk * WIDE + i * SET)

    @pl.when(pos >= 0)
    def _():
        for i in range(width // SET):
            sums_of(i * SET)

    q_copy.wait()


def head_kernel(count, pos_ref, seg_ref, edge_ref, halo_ref, early_ref, sw_ref, rate_ref, sum_ref, q_ref,
                total_ref, head_ref, use_ref, same_ref):
    pos = pos_ref[0]
    width = rate_ref.shape[1]
    per = count // LANES
    row = seg_ref[pl.ds(per * pos, 1), :]
    tail = seg_ref[pl.ds(per * pos + per - 1, 1), :]
    before = seg_ref[pl.ds(jnp.maximum(per * pos - 1, 0), 1), :]
    before = jnp.where(pos == 0, 0, before)
    s0, s1 = row[:, 0:1], row[:, 1:2]
    end = tail[:, LANES - 1 :]
    p1, p2 = before[:, LANES - 1 :], before[:, LANES - 2 : LANES - 1]
    same = lambda a, b: jnp.broadcast_to(flag(a == b), (1, width))
    near, far = same(p1, s0), same(p2, s0)
    step, skip = same(s0, s1), same(p1, s1)
    made = []
    for index in (0, 1, 2):
        h = jnp.where(pos == 0, early_ref[index].astype(F32), halo_ref[index].astype(F32))
        h2, h1 = h[0:1], h[1:2]
        w = [sw_ref[j, index : index + 1, :] for j in range(3)]
        if index == 0:
            use_ref[0:1, :] = w[1] * (near * h1) + w[2] * (far * h2)
            use_ref[1:2, :] = w[2] * (skip * h1)
            continue
        x0, x1 = edge_ref[2 * index - 2 : 2 * index - 1], edge_ref[2 * index - 1 : 2 * index]
        f0 = w[0] * x0 + w[1] * (near * h1) + w[2] * (far * h2)
        f1 = w[0] * x1 + w[1] * (step * x0) + w[2] * (skip * h1)
        made.append((f0, f1))
    u0 = (made[0][0] * made[1][0]).astype(BF).astype(F32)
    u1 = (made[0][1] * made[1][1]).astype(BF).astype(F32)
    head_ref[0:1, :] = u0
    head_ref[1:2, :] = u1
    u0 = same(s0, end) * u0
    u1 = same(s1, end) * u1
    half = width // 2
    for part in range(2):
        at = slice(part * half, (part + 1) * half)
        rate = rate_ref[:, at]
        drop = jnp.exp(-rate * (count - 2.0))
        total_ref[part] = (sum_ref[:, at] + drop * (u1[:, at] + jnp.exp(-rate) * u0[:, at])).astype(BF)


def plan_kernel(count, rounds, pos_ref, seg_ref, ids_ref, rates_ref, res_ref, rate_ref, col_ref,
                wide_ref, lead_ref, tri_ref, keep_ref, half_ref, full_ref):
    pos = pos_ref[0]
    modes = rates_ref.shape[0]
    width = rate_ref.shape[1]
    members = width // rates_ref.shape[1]

    def seg_at(spot):
        at = jnp.maximum(spot, 0)
        return jnp.where(spot < 0, 0, ids_ref[at])

    first = pos * count
    col = col_ref[1]
    start = iota((count, LANES), 0) // SUB
    lead = jnp.zeros((count, LANES), F32)
    for c in range(count // SUB):
        lead = jnp.where(start == c, seg_at(first + c * SUB - 1).astype(F32), lead)
    lead_ref[...] = flag(col == lead).astype(BF)
    inner = lax.rem(iota((SUB, SET), 1), SUB)
    tall = iota((SUB, SET), 0)
    for c in range(count // SUB):
        row = seg_ref[pl.ds((count // LANES) * pos + c * SUB // LANES, 1), :].astype(F32)
        shift = (c * SUB) % LANES
        base = row if shift == 0 else pltpu.roll(row, LANES - shift, 1)
        base = jnp.where(iota((1, LANES), 1) < SUB, base, 0.0)
        base = base + pltpu.roll(base, SUB, 1)
        base = base + pltpu.roll(base, 2 * SUB, 1)
        base = jnp.concatenate([base] * (SET // LANES), axis=1)
        mine = jnp.concatenate([col[c * SUB : (c + 1) * SUB]] * (SET // LANES), axis=1)
        tri_ref[c * SUB : (c + 1) * SUB, :] = flag((tall >= inner) & (mine == base)).astype(BF)
        keep_ref[c * modes : (c + 1) * modes, :] = jnp.broadcast_to(
            flag(base == ids_ref[first + (c + 1) * SUB - 1].astype(F32)), (modes, SET)).astype(BF)
    weight = res_ref[...] * jnp.sqrt(rates_ref[...])
    per = LANES * members
    onehot = flag(iota((LANES, per), 0) == iota((LANES, per), 1) // members).astype(BF)
    pick = iota((modes, per), 0) == lax.rem(iota((modes, per), 1), modes)
    for block in range(width // per):
        at = slice(block * LANES, (block + 1) * LANES)
        to = slice(block * per, (block + 1) * per)
        (spread,) = spread_out([weight[:, at]], onehot)
        wide_ref[:, to] = jnp.sum(jnp.where(pick, spread, 0.0), axis=0, keepdims=True)

    def decay(rate, low, high):
        alive = flag(seg_at(low * count - 1) == seg_at(high * count - 1))
        return jnp.exp(-rate * (count * (high - low)).astype(F32)) * alive

    core = lax.rem(pos, 2)
    chip = pos // 2
    rate = rate_ref[:, pl.ds(pl.multiple_of(core * (width // 2), LANES), width // 2)]
    half_ref[0] = decay(rate, 2 * chip + 1, 2 * chip + 2)
    spot = 1
    reach = 1
    for radix in rounds:
        size = reach * radix
        top = 2 * (chip // size) * size + 2 * size
        own = 2 * (chip // reach) * reach + 2 * reach
        half_ref[spot] = decay(rate, own, top)
        for other in range(1, radix):
            group = (chip // reach) ^ other
            finish = 2 * (group + 1) * reach
            ahead = group < chip // reach
            half_ref[spot + 1] = flag(ahead) * decay(rate, jnp.where(ahead, finish, 0), 2 * chip)
            half_ref[spot + 2] = decay(rate, finish, top)
            spot += 2
        spot += 1
        reach = size
    rate = rate_ref[...]
    full_ref[0] = jnp.where(core == 0, 1.0, decay(rate, 2 * chip, 2 * chip + 1))
    full_ref[1] = decay(rate, jnp.zeros_like(pos), pos)


def local_kernel(base, u_ref, head_ref, q_ref, halo_ref, sw_ref, skip_ref, rates_ref, res_ref, rate_ref, flat_ref,
                 wide_ref, lead_ref, col_ref, tri_ref, keep_ref, out_ref, gate_ref, cross_ref):
    count, wide = out_ref.shape
    modes = rates_ref.shape[0]
    members = 16
    groups = LANES // members
    spans = count // SUB
    first = base // members
    block = slice(first // LANES * LANES, first // LANES * LANES + LANES)
    cols = wide // members * SUB
    lane = iota((1, cols), 1)
    rates = rates_ref[:, block]
    weight = res_ref[:, block] * jnp.sqrt(rates)
    filt = lane // SUB + first % LANES
    onehot = flag(iota((LANES, cols), 0) == filt).astype(BF)
    (rate_to_end,) = spread_out([rates], onehot)
    decays = jnp.exp(-rate_to_end * (SUB - 1.0 - lax.rem(lane, SUB).astype(F32))).astype(BF)
    spot = lax.rem(lane, LANES)
    within = lax.rem((spot + SUB - 1) // SUB, LANES // SUB)
    lag = jnp.where(spot == 0, 0, lax.rem(SUB - lax.rem(spot, SUB), SUB)).astype(F32)
    filt = (lane // LANES) * (LANES // SUB) + within + first % LANES
    onehot = flag(iota((LANES, cols), 0) == filt).astype(BF)
    rate_tap, weight_tap = spread_out([rates, weight], onehot)
    taps = jnp.sum(weight_tap * jnp.exp(-rate_tap * lag), axis=0, keepdims=True)

    token = iota((16, LANES), 0)
    pad = lambda x, rows: jnp.concatenate([x, jnp.zeros((rows - x.shape[0], x.shape[1]), F32)], axis=0)
    owns = flag(iota((groups * SUB, LANES), 0) // SUB == iota((groups * SUB, LANES), 1) // members).astype(BF)
    holds = flag(iota((groups * modes, LANES), 0) // modes == iota((groups * modes, LANES), 1) // members).astype(BF)
    for tile in range(wide // LANES):
        at = slice(tile * LANES, (tile + 1) * LANES)
        to = slice(base + tile * LANES, base + (tile + 1) * LANES)
        ub = u_ref[:, to]
        start = jnp.where(token < 2, pad(head_ref[:, to], 16), ub[:16].astype(F32)).astype(BF)
        ub = jnp.concatenate([start, ub[16:]], axis=0)
        rflat, wflat = flat_ref[:, to], wide_ref[:, to]
        near = []
        for part in range(SET // LANES):
            row = taps[:, tile * SET + part * LANES : tile * SET + (part + 1) * LANES]
            near.append(pltpu.roll(jnp.broadcast_to(row, (SUB, LANES)), 0, 1, stride=1, stride_axis=0))
        near = jnp.concatenate(near, axis=1).astype(BF)
        ends = decays[:, tile * SET : (tile + 1) * SET]
        table = wflat * jnp.exp(-rflat * (iota((SUB, LANES), 0).astype(F32) + 1.0))
        fall = jnp.exp(-rate_ref[:, to] * float(SUB))
        far = jnp.exp(-rflat * (SUB * iota((spans, LANES), 0).astype(F32)))
        inner, sums = [], []
        for c in range(spans):
            rows = slice(c * SUB, (c + 1) * SUB)
            left = jnp.concatenate([near * tri_ref[rows], ends * keep_ref[c * 16 : (c + 1) * 16]], axis=0)
            right = jnp.concatenate([ub[rows]] * groups, axis=0) * owns
            got = jnp.dot(left, right, preferred_element_type=F32)
            inner.append(got[:SUB])
            sums.append(got[SUB:])
            cross_ref[rows, at] = (table * far[c : c + 1] * col_ref[0, rows]).astype(BF)
        tableb = table.astype(BF)
        state = sums[0]
        local = [inner[0]]
        for c in range(1, spans):
            rows = slice(c * SUB, (c + 1) * SUB)
            reach = lead_ref[rows].astype(F32)
            right = jnp.concatenate([state.astype(BF)] * groups, axis=0) * holds
            local.append(inner[c] + jnp.dot(tableb * lead_ref[rows], right, preferred_element_type=F32))
            state = fall * reach[SUB - 1 :] * state + sums[c]
        x = q_ref[:, to].astype(F32)
        q = (
            sw_ref[0, 0:1, to] * x
            + sw_ref[1, 0:1, to] * (col_ref[2] * pltpu.roll(x, 1, 0))
            + sw_ref[2, 0:1, to] * (col_ref[3] * pltpu.roll(x, 2, 0))
        )
        q = jnp.concatenate([q[:8] + pad(halo_ref[:, to], 8), q[8:]], axis=0)
        gate_ref[:, at] = q
        out_ref[:, at] = q * (jnp.concatenate(local, axis=0) + skip_ref[:, to] * ub.astype(F32))


def last_kernel(pieces, state_ref, *refs):
    modes = state_ref.shape[0]
    members = 16
    groups = SET // members
    owner = iota((modes, SET), 1) // members
    out_ref, made_ref, sems = refs[3 * pieces :]
    copies = []
    for piece in range(pieces):
        part_ref, gate_ref, table_ref = refs[3 * piece : 3 * piece + 3]
        wide = part_ref.shape[1]
        for half in range(wide // SET):
            at = slice(half * SET, (half + 1) * SET)
            to = slice(piece * wide + half * SET, piece * wide + (half + 1) * SET)
            state = state_ref[:, to]
            spread = jnp.concatenate([jnp.where(owner == g, state, 0.0).astype(BF) for g in range(groups)], axis=0)
            cross = jnp.dot(table_ref[:, at], spread, preferred_element_type=F32)
            made_ref[:, to] = (part_ref[:, at] + gate_ref[:, at] * cross).astype(BF)
        to = slice(piece * wide, (piece + 1) * wide)
        copies.append(pltpu.make_async_copy(made_ref.at[:, to], out_ref.at[:, to], sems.at[piece]))
        copies[-1].start()
    for copy in copies:
        copy.wait()


def params(limit=16 << 20):
    return pltpu.CompilerParams(vmem_limit_bytes=limit)


def body(features, short_weight, residues, rates, skip, carry_state, earlier_rows, segment_ids):
    count, _, width = features.shape
    groups, modes = rates.shape
    blocks = lax.axis_size("ctx")
    pos = lax.axis_index("ctx")
    pos1 = pos.reshape(1)
    chips = blocks // 2
    bits = chips.bit_length() - 1
    rounds = ([4] if bits > 1 else []) + [2] * (bits - 2 if bits > 1 else bits)
    assert blocks == 2 << bits and count == 2 * LANES and width == 16 * groups and modes == 16
    feat = jnp.transpose(features, (1, 0, 2))
    early = jnp.transpose(earlier_rows, (1, 0, 2))
    segs = segment_ids.reshape(-1, LANES)
    rates_t = rates.T
    res_t = residues.T
    skip = skip.reshape(1, width)
    vm = pl.BlockSpec(memory_space=pltpu.VMEM)
    sm = pl.BlockSpec(memory_space=pltpu.SMEM)
    out = lambda *shape, dtype=F32: jax.ShapeDtypeStruct(shape, dtype)
    stay = lambda value: pltpu.with_memory_space_constraint(value, pltpu.HBM)
    swap = lambda value, by: lax.ppermute(value, "ctx", [(i, i ^ by) for i in range(blocks)])
    tie = lambda *values: lax.optimization_barrier(values)

    halo = lax.ppermute(feat[:, count - 2 :], "ctx", [(i, i + 1) for i in range(blocks - 1)])

    hbm = pl.BlockSpec(memory_space=pltpu.HBM)
    u, q, sums, rate, flat, edge, cols, weights = pl.pallas_call(
        first_kernel,
        in_specs=[sm, hbm, hbm, hbm, hbm],
        out_specs=[vm] * 8,
        out_shape=[out(count, width, dtype=BF), out(count, width, dtype=BF), out(modes, width), out(modes, width),
                   out(1, width), out(4, width), out(4, count, LANES),
                   out(*short_weight.shape)],
        scratch_shapes=[
            pltpu.VMEM((count, LANES), BF), pltpu.VMEM((2 * count, count), BF), pltpu.VMEM((2, count, width), BF), pltpu.VMEM(segs.shape, jnp.int32),
            pltpu.VMEM(rates_t.shape, F32), pltpu.SemaphoreType.DMA((2 * (width // WIDE) + 4,)),
        ],
        compiler_params=params(),
        name="first",
    )(pos1, stay(segs), stay(rates_t), stay(feat), stay(short_weight))

    total, head, halo_q, q = pl.pallas_call(
        lambda *refs: head_kernel(count, *refs),
        in_specs=[sm] + [vm] * 8,
        out_specs=[vm] * 4,
        out_shape=[out(2, modes, width // 2, dtype=BF), out(2, width), out(2, width), out(count, width, dtype=BF)],
        input_output_aliases={8: 3},
        compiler_params=params(),
        name="head",
    )(pos1, segs, edge, halo, early, weights, rate, sums, q)

    even = (pos & 1) == 0
    other = swap(total, 1)
    steps = 1 + sum(2 * radix - 1 for radix in rounds)
    wflat, lead, tris, keeps, halves, fulls = pl.pallas_call(
        lambda *refs: plan_kernel(count, rounds, *refs),
        in_specs=[sm, vm, sm] + [vm] * 4,
        out_specs=[vm] * 6,
        out_shape=[
            out(1, width), out(count, LANES, dtype=BF), out(count, SET, dtype=BF), out(count // SUB * 16, SET, dtype=BF),
            out(steps, modes, width // 2), out(2, modes, width),
        ],
        compiler_params=params(),
        cost_estimate=pl.CostEstimate(flops=1 << 30, bytes_accessed=5 << 20, transcendentals=0),
        name="plan",
    )(pos1, segs, segment_ids, rates_t, res_t, rate, cols)

    pieces = width // PIECE
    parts = []

    def local(piece, head):
        return pl.pallas_call(
            lambda *refs: local_kernel(piece * PIECE, *refs),
            in_specs=[vm] * 15,
            out_specs=[vm] * 3,
            out_shape=[out(count, PIECE), out(count, PIECE), out(count, PIECE, dtype=BF)],
            compiler_params=params(),
            cost_estimate=pl.CostEstimate(flops=4 << 30, bytes_accessed=5 << 20, transcendentals=0),
            name="local",
        )(u, head, q, halo_q, weights, skip, rates_t, res_t, rate, flat, wflat, lead, cols, tris, keeps)

    low_total = jnp.where(even, total, other)
    own_half = lambda value: jnp.where(even, value[0], value[1]).astype(F32)
    chip_total = halves[0] * own_half(low_total) + own_half(jnp.where(even, other, total))
    chip_total, head = tie(chip_total, head)
    before = jnp.zeros_like(chip_total)
    spot, reach = 1, 1
    left = list(range(pieces))
    for number, radix in enumerate(rounds):
        sent = chip_total.astype(BF)
        got = [swap(sent, 2 * reach * i).astype(F32) for i in range(1, radix)]
        share = -(-len(left) // (len(rounds) - number))
        for piece in left[:share]:
            parts.append(local(piece, head))
        left = left[share:]
        got, parts, head = tie(got, parts, head)
        chip_total = halves[spot] * chip_total
        for i in range(radix - 1):
            before = before + halves[spot + 1 + 2 * i] * got[i]
            chip_total = chip_total + halves[spot + 2 + 2 * i] * got[i]
        spot += 2 * radix - 1
        reach *= radix
    mine = before.astype(BF)
    yours = swap(mine, 1)
    full = jnp.concatenate([jnp.where(even, mine, yours), jnp.where(even, yours, mine)], axis=1).astype(F32)
    low_full = jnp.where(even, 0.0, jnp.concatenate([low_total[0], low_total[1]], axis=1).astype(F32))
    state = fulls[0] * full + low_full + fulls[1] * carry_state

    return pl.pallas_call(
        lambda *refs: last_kernel(pieces, *refs),
        in_specs=[vm] * (1 + 3 * pieces),
        out_specs=hbm,
        out_shape=out(count, width, dtype=BF),
        scratch_shapes=[pltpu.VMEM((count, width), BF), pltpu.SemaphoreType.DMA((pieces,))],
        compiler_params=params(),
        name="last",
    )(state, *[value for piece in parts for value in piece])


def solution(mesh):
    placed = (
        P(("groups", "ctx"), None, None),
        P(),
        P(),
        P(),
        P(),
        P("groups", None),
        P("groups", None, None),
        P("groups"),
    )
    return jax.shard_map(
        body, mesh=mesh, in_specs=placed, out_specs=P(("groups", "ctx"), None), check_vma=False
    )
```

```python
import jax
import jax.numpy as jnp
from jax import lax
from jax.experimental import pallas as pl
from jax.experimental.pallas import tpu as pltpu
from jax.sharding import PartitionSpec as P

BF = jnp.bfloat16
F32 = jnp.float32
LANES = 128
SET = 256
WIDE = 1024
PIECE = 2048
SUB = 32


def iota(shape, dim):
    return lax.broadcasted_iota(jnp.int32, shape, dim)


def flag(x):
    return x.astype(F32)


def split3(x):
    hi = x.astype(BF)
    rest = x - hi.astype(F32)
    mid = rest.astype(BF)
    low = (rest - mid.astype(F32)).astype(BF)
    return [hi, mid, low]


def spread_out(values, onehot):
    rows = values[0].shape[0]
    pieces = sum([split3(value) for value in values], [])
    got = jnp.dot(jnp.concatenate(pieces, axis=0), onehot, preferred_element_type=F32)
    part = lambda i: got[i * rows : (i + 1) * rows]
    return [(part(3 * i) + part(3 * i + 1)) + part(3 * i + 2) for i in range(len(values))]


def first_kernel(pos_ref, seg_hbm, rates_hbm, feat_ref, taps_hbm,
                 u_ref, sum_ref, rate_ref, flat_ref, edge_ref, col_ref, taps_ref,
                 keep_ref, shift_ref, kv_ref, seg_ref, rates_ref, sems):
    pos = pos_ref[0]
    count, width = u_ref.shape
    modes = sum_ref.shape[0]
    members = SET // modes
    chunks = width // WIDE

    def copies(chunk):
        at = slice(chunk * WIDE, (chunk + 1) * WIDE)
        return [
            pltpu.make_async_copy(feat_ref.at[1 + i, :, at], kv_ref.at[i, :, at], sems.at[2 * chunk + i])
            for i in range(2)
        ]

    small = [
        pltpu.make_async_copy(source, target, sems.at[2 * chunks + i])
        for i, (source, target) in enumerate(((seg_hbm, seg_ref), (rates_hbm, rates_ref), (taps_hbm, taps_ref)))
    ]
    for copy in small:
        copy.start()
    for chunk in range(chunks):
        for copy in copies(chunk):
            copy.start()
    for copy in small:
        copy.wait()

    @pl.when(pos >= 0)
    def _():
        token = iota((count, LANES), 0)
        halves, rows = [], []
        for part in range(count // LANES):
            row = seg_ref[pl.ds((count // LANES) * pos + part, 1), :].astype(F32)
            rows.append(row)
            halves.append(jnp.transpose(jnp.broadcast_to(row, (LANES, LANES))))
        col = jnp.concatenate(halves, axis=0)
        before = seg_ref[pl.ds(jnp.maximum((count // LANES) * pos - 1, 0), 1), :].astype(F32)
        before = jnp.where(pos == 0, 0.0, before)
        last = jnp.broadcast_to(before[:, LANES - 1 :], (1, LANES))
        end = jnp.broadcast_to(rows[-1][:, LANES - 1 :], (1, LANES))
        col_ref[0] = flag(col == last)
        col_ref[1] = col
        keep_ref[...] = flag((col == end) & (token >= 2)).astype(BF)
        col_ref[2] = flag((col == pltpu.roll(col, 1, 0)) & (token >= 1))
        col_ref[3] = flag((col == pltpu.roll(col, 2, 0)) & (token >= 2))
        every = jnp.concatenate(rows, axis=1)
        there = jnp.concatenate([col] * (count // LANES), axis=1)
        gap = iota((count, count), 0) - iota((count, count), 1)
        for step in (1, 2):
            shift_ref[(step - 1) * count : step * count, :] = flag((gap == step) & (there == every)).astype(BF)

        per = LANES * members
        onehot = flag(iota((LANES, per), 0) == iota((LANES, per), 1) // members).astype(BF)
        pick = iota((modes, per), 0) == lax.rem(iota((modes, per), 1), modes)
        for block in range(width // per):
            at = slice(block * LANES, (block + 1) * LANES)
            to = slice(block * per, (block + 1) * per)
            (rate,) = spread_out([rates_ref[:, at]], onehot)
            rate_ref[:, to] = rate
            flat_ref[:, to] = jnp.sum(jnp.where(pick, rate, 0.0), axis=0, keepdims=True)

    owner = iota((modes, LANES), 1) // members
    spans = count // SUB

    def two_tiles(start):
        both = pl.ds(start, SET)
        shifted = []
        for index in (1, 2):
            edge_ref[2 * index - 2 : 2 * index, both] = kv_ref[index - 1, :16, both].astype(F32)[:2]
            shifted.append(jnp.dot(shift_ref[...], kv_ref[index - 1, :, both], preferred_element_type=F32))
        for part in range(SET // LANES):
            at = pl.ds(start + part * LANES, LANES)
            cut = slice(part * LANES, (part + 1) * LANES)
            made = []
            for index in (1, 2):
                moved = shifted[index - 1]
                made.append(
                    taps_ref[0, index : index + 1, at] * kv_ref[index - 1, :, at].astype(F32)
                    + taps_ref[1, index : index + 1, at] * moved[:count, cut]
                    + taps_ref[2, index : index + 1, at] * moved[count:, cut]
                )
            u = (made[0] * made[1]).astype(BF)
            u_ref[:, at] = u

    def sums_of(start):
        at = pl.ds(start, SET)
        rflat = flat_ref[:, at]
        fine = jnp.exp(-rflat * (SUB - 1.0 - iota((SUB, SET), 0).astype(F32)))
        coarse = jnp.exp(-rflat * (SUB * (spans - 1.0 - iota((spans, SET), 0).astype(F32))))
        decay = jnp.concatenate([(coarse[a : a + 1] * fine).astype(BF) for a in range(spans)], axis=0)
        decay = decay * jnp.concatenate([keep_ref[...]] * (SET // LANES), axis=1)
        sums = lax.dot_general(decay, u_ref[:, at], (((0,), (0,)), ((), ())), preferred_element_type=F32)
        for part in range(SET // LANES):
            cut = slice(part * LANES, (part + 1) * LANES)
            total = jnp.zeros((modes, LANES), F32)
            for g in range(LANES // members):
                row = part * LANES + g * modes
                total = jnp.where(owner == g, sums[row : row + modes, cut], total)
            sum_ref[:, pl.ds(start + part * LANES, LANES)] = total

    for chunk in range(chunks):
        for copy in copies(chunk):
            copy.wait()

        @pl.when(pos >= 0)
        def _():
            for i in range(WIDE // SET):
                two_tiles(chunk * WIDE + i * SET)

    @pl.when(pos >= 0)
    def _():
        for i in range(width // SET):
            sums_of(i * SET)


def head_kernel(count, pos_ref, seg_ref, edge_ref, halo_ref, early_ref, sw_ref, rate_ref, sum_ref,
                total_ref, head_ref, use_ref):
    pos = pos_ref[0]
    width = rate_ref.shape[1]
    per = count // LANES
    row = seg_ref[pl.ds(per * pos, 1), :]
    tail = seg_ref[pl.ds(per * pos + per - 1, 1), :]
    before = seg_ref[pl.ds(jnp.maximum(per * pos - 1, 0), 1), :]
    before = jnp.where(pos == 0, 0, before)
    s0, s1 = row[:, 0:1], row[:, 1:2]
    end = tail[:, LANES - 1 :]
    p1, p2 = before[:, LANES - 1 :], before[:, LANES - 2 : LANES - 1]
    same = lambda a, b: jnp.broadcast_to(flag(a == b), (1, width))
    near, far = same(p1, s0), same(p2, s0)
    step, skip = same(s0, s1), same(p1, s1)
    made = []
    for index in (0, 1, 2):
        h = jnp.where(pos == 0, early_ref[index].astype(F32), halo_ref[index].astype(F32))
        h2, h1 = h[0:1], h[1:2]
        w = [sw_ref[j, index : index + 1, :] for j in range(3)]
        if index == 0:
            use_ref[0:1, :] = w[1] * (near * h1) + w[2] * (far * h2)
            use_ref[1:2, :] = w[2] * (skip * h1)
            continue
        x0, x1 = edge_ref[2 * index - 2 : 2 * index - 1], edge_ref[2 * index - 1 : 2 * index]
        f0 = w[0] * x0 + w[1] * (near * h1) + w[2] * (far * h2)
        f1 = w[0] * x1 + w[1] * (step * x0) + w[2] * (skip * h1)
        made.append((f0, f1))
    u0 = (made[0][0] * made[1][0]).astype(BF).astype(F32)
    u1 = (made[0][1] * made[1][1]).astype(BF).astype(F32)
    head_ref[0:1, :] = u0
    head_ref[1:2, :] = u1
    u0 = same(s0, end) * u0
    u1 = same(s1, end) * u1
    half = width // 2
    for part in range(2):
        at = slice(part * half, (part + 1) * half)
        rate = rate_ref[:, at]
        drop = jnp.exp(-rate * (count - 2.0))
        total_ref[part] = (sum_ref[:, at] + drop * (u1[:, at] + jnp.exp(-rate) * u0[:, at])).astype(BF)


def plan_kernel(count, rounds, pos_ref, seg_ref, ids_ref, rates_ref, res_ref, rate_ref, col_ref, feat_ref,
                wide_ref, lead_ref, tri_ref, keep_ref, half_ref, full_ref, q_ref, sem):
    q_copies = [
        pltpu.make_async_copy(feat_ref.at[0, i * 32 : (i + 1) * 32], q_ref.at[i * 32 : (i + 1) * 32], sem.at[i])
        for i in range(count // 32)
    ]
    for copy in q_copies:
        copy.start()
    pos = pos_ref[0]

    @pl.when(pos >= 0)
    def _():
        modes = rates_ref.shape[0]
        width = rate_ref.shape[1]
        members = width // rates_ref.shape[1]

        def seg_at(spot):
            at = jnp.maximum(spot, 0)
            return jnp.where(spot < 0, 0, ids_ref[at])

        first = pos * count
        col = col_ref[1]
        start = iota((count, LANES), 0) // SUB
        lead = jnp.zeros((count, LANES), F32)
        for c in range(count // SUB):
            lead = jnp.where(start == c, seg_at(first + c * SUB - 1).astype(F32), lead)
        lead_ref[...] = flag(col == lead).astype(BF)
        inner = lax.rem(iota((SUB, SET), 1), SUB)
        tall = iota((SUB, SET), 0)
        for c in range(count // SUB):
            row = seg_ref[pl.ds((count // LANES) * pos + c * SUB // LANES, 1), :].astype(F32)
            shift = (c * SUB) % LANES
            base = row if shift == 0 else pltpu.roll(row, LANES - shift, 1)
            base = jnp.where(iota((1, LANES), 1) < SUB, base, 0.0)
            base = base + pltpu.roll(base, SUB, 1)
            base = base + pltpu.roll(base, 2 * SUB, 1)
            base = jnp.concatenate([base] * (SET // LANES), axis=1)
            mine = jnp.concatenate([col[c * SUB : (c + 1) * SUB]] * (SET // LANES), axis=1)
            tri_ref[c * SUB : (c + 1) * SUB, :] = flag((tall >= inner) & (mine == base)).astype(BF)
            keep_ref[c * modes : (c + 1) * modes, :] = jnp.broadcast_to(
                flag(base == ids_ref[first + (c + 1) * SUB - 1].astype(F32)), (modes, SET)).astype(BF)
        weight = res_ref[...] * jnp.sqrt(rates_ref[...])
        per = LANES * members
        onehot = flag(iota((LANES, per), 0) == iota((LANES, per), 1) // members).astype(BF)
        pick = iota((modes, per), 0) == lax.rem(iota((modes, per), 1), modes)
        for block in range(width // per):
            at = slice(block * LANES, (block + 1) * LANES)
            to = slice(block * per, (block + 1) * per)
            (spread,) = spread_out([weight[:, at]], onehot)
            wide_ref[:, to] = jnp.sum(jnp.where(pick, spread, 0.0), axis=0, keepdims=True)

        def decay(rate, low, high):
            alive = flag(seg_at(low * count - 1) == seg_at(high * count - 1))
            return jnp.exp(-rate * (count * (high - low)).astype(F32)) * alive

        core = lax.rem(pos, 2)
        chip = pos // 2
        rate = rate_ref[:, pl.ds(pl.multiple_of(core * (width // 2), LANES), width // 2)]
        half_ref[0] = decay(rate, 2 * chip + 1, 2 * chip + 2)
        spot = 1
        reach = 1
        for radix in rounds:
            size = reach * radix
            top = 2 * (chip // size) * size + 2 * size
            own = 2 * (chip // reach) * reach + 2 * reach
            half_ref[spot] = decay(rate, own, top)
            for other in range(1, radix):
                group = (chip // reach) ^ other
                finish = 2 * (group + 1) * reach
                ahead = group < chip // reach
                half_ref[spot + 1] = flag(ahead) * decay(rate, jnp.where(ahead, finish, 0), 2 * chip)
                half_ref[spot + 2] = decay(rate, finish, top)
                spot += 2
            spot += 1
            reach = size
        rate = rate_ref[...]
        full_ref[0] = jnp.where(core == 0, 1.0, decay(rate, 2 * chip, 2 * chip + 1))
        full_ref[1] = decay(rate, jnp.zeros_like(pos), pos)

    for copy in q_copies:
        copy.wait()


def local_kernel(base, u_ref, head_ref, q_ref, halo_ref, sw_ref, skip_ref, rates_ref, res_ref, rate_ref, flat_ref,
                 wide_ref, lead_ref, col_ref, tri_ref, keep_ref, out_ref, gate_ref, cross_ref):
    count, wide = out_ref.shape
    modes = rates_ref.shape[0]
    members = 16
    groups = LANES // members
    spans = count // SUB
    first = base // members
    block = slice(first // LANES * LANES, first // LANES * LANES + LANES)
    cols = wide // members * SUB
    lane = iota((1, cols), 1)
    rates = rates_ref[:, block]
    weight = res_ref[:, block] * jnp.sqrt(rates)
    filt = lane // SUB + first % LANES
    onehot = flag(iota((LANES, cols), 0) == filt).astype(BF)
    (rate_to_end,) = spread_out([rates], onehot)
    decays = jnp.exp(-rate_to_end * (SUB - 1.0 - lax.rem(lane, SUB).astype(F32))).astype(BF)
    spot = lax.rem(lane, LANES)
    within = lax.rem((spot + SUB - 1) // SUB, LANES // SUB)
    lag = jnp.where(spot == 0, 0, lax.rem(SUB - lax.rem(spot, SUB), SUB)).astype(F32)
    filt = (lane // LANES) * (LANES // SUB) + within + first % LANES
    onehot = flag(iota((LANES, cols), 0) == filt).astype(BF)
    rate_tap, weight_tap = spread_out([rates, weight], onehot)
    taps = jnp.sum(weight_tap * jnp.exp(-rate_tap * lag), axis=0, keepdims=True)

    token = iota((16, LANES), 0)
    pad = lambda x, rows: jnp.concatenate([x, jnp.zeros((rows - x.shape[0], x.shape[1]), F32)], axis=0)
    owns = flag(iota((groups * SUB, LANES), 0) // SUB == iota((groups * SUB, LANES), 1) // members).astype(BF)
    holds = flag(iota((groups * modes, LANES), 0) // modes == iota((groups * modes, LANES), 1) // members).astype(BF)
    for tile in range(wide // LANES):
        at = slice(tile * LANES, (tile + 1) * LANES)
        to = slice(base + tile * LANES, base + (tile + 1) * LANES)
        ub = u_ref[:, to]
        start = jnp.where(token < 2, pad(head_ref[:, to], 16), ub[:16].astype(F32)).astype(BF)
        ub = jnp.concatenate([start, ub[16:]], axis=0)
        rflat, wflat = flat_ref[:, to], wide_ref[:, to]
        near = []
        for part in range(SET // LANES):
            row = taps[:, tile * SET + part * LANES : tile * SET + (part + 1) * LANES]
            near.append(pltpu.roll(jnp.broadcast_to(row, (SUB, LANES)), 0, 1, stride=1, stride_axis=0))
        near = jnp.concatenate(near, axis=1).astype(BF)
        ends = decays[:, tile * SET : (tile + 1) * SET]
        table = wflat * jnp.exp(-rflat * (iota((SUB, LANES), 0).astype(F32) + 1.0))
        fall = jnp.exp(-rate_ref[:, to] * float(SUB))
        far = jnp.exp(-rflat * (SUB * iota((spans, LANES), 0).astype(F32)))
        inner, sums = [], []
        for c in range(spans):
            rows = slice(c * SUB, (c + 1) * SUB)
            left = jnp.concatenate([near * tri_ref[rows], ends * keep_ref[c * 16 : (c + 1) * 16]], axis=0)
            right = jnp.concatenate([ub[rows]] * groups, axis=0) * owns
            got = jnp.dot(left, right, preferred_element_type=F32)
            inner.append(got[:SUB])
            sums.append(got[SUB:])
            cross_ref[rows, at] = (table * far[c : c + 1] * col_ref[0, rows]).astype(BF)
        tableb = table.astype(BF)
        state = sums[0]
        local = [inner[0]]
        for c in range(1, spans):
            rows = slice(c * SUB, (c + 1) * SUB)
            reach = lead_ref[rows].astype(F32)
            right = jnp.concatenate([state.astype(BF)] * groups, axis=0) * holds
            local.append(inner[c] + jnp.dot(tableb * lead_ref[rows], right, preferred_element_type=F32))
            state = fall * reach[SUB - 1 :] * state + sums[c]
        x = q_ref[:, to].astype(F32)
        q = (
            sw_ref[0, 0:1, to] * x
            + sw_ref[1, 0:1, to] * (col_ref[2] * pltpu.roll(x, 1, 0))
            + sw_ref[2, 0:1, to] * (col_ref[3] * pltpu.roll(x, 2, 0))
        )
        q = jnp.concatenate([q[:8] + pad(halo_ref[:, to], 8), q[8:]], axis=0)
        gate_ref[:, at] = q
        out_ref[:, at] = q * (jnp.concatenate(local, axis=0) + skip_ref[:, to] * ub.astype(F32))


def last_kernel(pieces, state_ref, *refs):
    modes = state_ref.shape[0]
    members = 16
    groups = SET // members
    owner = iota((modes, SET), 1) // members
    out_ref, made_ref, sems = refs[3 * pieces :]
    copies = []
    for piece in range(pieces):
        part_ref, gate_ref, table_ref = refs[3 * piece : 3 * piece + 3]
        wide = part_ref.shape[1]
        for half in range(wide // SET):
            at = slice(half * SET, (half + 1) * SET)
            to = slice(piece * wide + half * SET, piece * wide + (half + 1) * SET)
            state = state_ref[:, to]
            spread = jnp.concatenate([jnp.where(owner == g, state, 0.0).astype(BF) for g in range(groups)], axis=0)
            cross = jnp.dot(table_ref[:, at], spread, preferred_element_type=F32)
            made_ref[:, to] = (part_ref[:, at] + gate_ref[:, at] * cross).astype(BF)
        to = slice(piece * wide, (piece + 1) * wide)
        copies.append(pltpu.make_async_copy(made_ref.at[:, to], out_ref.at[:, to], sems.at[piece]))
        copies[-1].start()
    for copy in copies:
        copy.wait()


def params(limit=16 << 20):
    return pltpu.CompilerParams(vmem_limit_bytes=limit)


def body(features, short_weight, residues, rates, skip, carry_state, earlier_rows, segment_ids):
    count, _, width = features.shape
    groups, modes = rates.shape
    blocks = lax.axis_size("ctx")
    pos = lax.axis_index("ctx")
    pos1 = pos.reshape(1)
    chips = blocks // 2
    bits = chips.bit_length() - 1
    rounds = ([4] if bits > 1 else []) + [2] * (bits - 2 if bits > 1 else bits)
    assert blocks == 2 << bits and count == 2 * LANES and width == 16 * groups and modes == 16
    feat = jnp.transpose(features, (1, 0, 2))
    early = jnp.transpose(earlier_rows, (1, 0, 2))
    segs = segment_ids.reshape(-1, LANES)
    rates_t = rates.T
    res_t = residues.T
    skip = skip.reshape(1, width)
    vm = pl.BlockSpec(memory_space=pltpu.VMEM)
    sm = pl.BlockSpec(memory_space=pltpu.SMEM)
    out = lambda *shape, dtype=F32: jax.ShapeDtypeStruct(shape, dtype)
    stay = lambda value: pltpu.with_memory_space_constraint(value, pltpu.HBM)
    swap = lambda value, by: lax.ppermute(value, "ctx", [(i, i ^ by) for i in range(blocks)])
    tie = lambda *values: lax.optimization_barrier(values)

    halo = lax.ppermute(feat[:, count - 2 :], "ctx", [(i, i + 1) for i in range(blocks - 1)])

    hbm = pl.BlockSpec(memory_space=pltpu.HBM)
    u, sums, rate, flat, edge, cols, weights = pl.pallas_call(
        first_kernel,
        in_specs=[sm, hbm, hbm, hbm, hbm],
        out_specs=[vm] * 7,
        out_shape=[out(count, width, dtype=BF), out(modes, width), out(modes, width),
                   out(1, width), out(4, width), out(4, count, LANES),
                   out(*short_weight.shape)],
        scratch_shapes=[
            pltpu.VMEM((count, LANES), BF), pltpu.VMEM((2 * count, count), BF), pltpu.VMEM((2, count, width), BF), pltpu.VMEM(segs.shape, jnp.int32),
            pltpu.VMEM(rates_t.shape, F32), pltpu.SemaphoreType.DMA((2 * (width // WIDE) + 3,)),
        ],
        compiler_params=params(),
        name="first",
    )(pos1, stay(segs), stay(rates_t), stay(feat), stay(short_weight))

    total, head, halo_q = pl.pallas_call(
        lambda *refs: head_kernel(count, *refs),
        in_specs=[sm] + [vm] * 7,
        out_specs=[vm] * 3,
        out_shape=[out(2, modes, width // 2, dtype=BF), out(2, width), out(2, width)],
        compiler_params=params(),
        name="head",
    )(pos1, segs, edge, halo, early, weights, rate, sums)

    even = (pos & 1) == 0
    other = swap(total, 1)
    steps = 1 + sum(2 * radix - 1 for radix in rounds)
    wflat, lead, tris, keeps, halves, fulls, q = pl.pallas_call(
        lambda *refs: plan_kernel(count, rounds, *refs),
        in_specs=[sm, vm, sm] + [vm] * 4 + [hbm],
        out_specs=[vm] * 7,
        out_shape=[
            out(1, width), out(count, LANES, dtype=BF), out(count, SET, dtype=BF), out(count // SUB * 16, SET, dtype=BF),
            out(steps, modes, width // 2), out(2, modes, width), out(count, width, dtype=BF),
        ],
        scratch_shapes=[pltpu.SemaphoreType.DMA((count // 32,))],
        compiler_params=params(),
        cost_estimate=pl.CostEstimate(flops=1 << 30, bytes_accessed=5 << 20, transcendentals=0),
        name="plan",
    )(pos1, segs, segment_ids, rates_t, res_t, rate, cols, stay(feat))

    pieces = width // PIECE
    parts = []

    def local(piece, head):
        return pl.pallas_call(
            lambda *refs: local_kernel(piece * PIECE, *refs),
            in_specs=[vm] * 15,
            out_specs=[vm] * 3,
            out_shape=[out(count, PIECE), out(count, PIECE), out(count, PIECE, dtype=BF)],
            compiler_params=params(),
            cost_estimate=pl.CostEstimate(flops=4 << 30, bytes_accessed=5 << 20, transcendentals=0),
            name="local",
        )(u, head, q, halo_q, weights, skip, rates_t, res_t, rate, flat, wflat, lead, cols, tris, keeps)

    low_total = jnp.where(even, total, other)
    own_half = lambda value: jnp.where(even, value[0], value[1]).astype(F32)
    chip_total = halves[0] * own_half(low_total) + own_half(jnp.where(even, other, total))
    chip_total, head = tie(chip_total, head)
    before = jnp.zeros_like(chip_total)
    spot, reach = 1, 1
    left = list(range(pieces))
    for number, radix in enumerate(rounds):
        sent = chip_total.astype(BF)
        got = [swap(sent, 2 * reach * i).astype(F32) for i in range(1, radix)]
        share = -(-len(left) // (len(rounds) - number))
        for piece in left[:share]:
            parts.append(local(piece, head))
        left = left[share:]
        got, parts, head = tie(got, parts, head)
        chip_total = halves[spot] * chip_total
        for i in range(radix - 1):
            before = before + halves[spot + 1 + 2 * i] * got[i]
            chip_total = chip_total + halves[spot + 2 + 2 * i] * got[i]
        spot += 2 * radix - 1
        reach *= radix
    mine = before.astype(BF)
    yours = swap(mine, 1)
    full = jnp.concatenate([jnp.where(even, mine, yours), jnp.where(even, yours, mine)], axis=1).astype(F32)
    low_full = jnp.where(even, 0.0, jnp.concatenate([low_total[0], low_total[1]], axis=1).astype(F32))
    state = fulls[0] * full + low_full + fulls[1] * carry_state

    return pl.pallas_call(
        lambda *refs: last_kernel(pieces, *refs),
        in_specs=[vm] * (1 + 3 * pieces),
        out_specs=hbm,
        out_shape=out(count, width, dtype=BF),
        scratch_shapes=[pltpu.VMEM((count, width), BF), pltpu.SemaphoreType.DMA((pieces,))],
        compiler_params=params(),
        name="last",
    )(state, *[value for piece in parts for value in piece])


def solution(mesh):
    placed = (
        P(("groups", "ctx"), None, None),
        P(),
        P(),
        P(),
        P(),
        P("groups", None),
        P("groups", None, None),
        P("groups"),
    )
    return jax.shard_map(
        body, mesh=mesh, in_specs=placed, out_specs=P(("groups", "ctx"), None), check_vma=False
    )
```
